32 devices in a mesh: tm: 8 (over z, x), head: 4 (over y, core).
Axes of the slice: x: 2, y: 2, z: 4, core: 2. Of those that a mesh axis runs over, the one named last changes fastest.
Arguments:
- query_vectors: bfloat16 [4096, 5120], P('tm', 'head'), may hold values from -10 to 10
- key_vectors: bfloat16 [4096, 5120], P('tm', 'head'), may hold values from -4 to 4
- value_vectors: bfloat16 [4096, 5120], P('tm', 'head'), may hold values from -8 to 8
- band_table: int32 [8, 8], replicated, may hold values from 0 to 4, as said below
- out_weight: bfloat16 [5120, 5120], P('head'), may hold values from -0.078125 to 0.078125
Outputs:
- block_output: bfloat16 [4096, 5120], P('tm', 'head')
The draws below stay inside these ranges and needn't reach their ends.
Inputs may be any that keep to these rules, and one draw needn't show every extreme that they name: band_table[t][t] is 0; for t != s it is b or b + 1, where b is the number of binary digits of |t - s|.
All inputs are finite; a program needn't handle non-finite values.
Results may differ from the reference program's by a relative error of at most 0.012.
Values may be sent and summed in bfloat16 or wider, within the bound.
No kernel may reach another device: no remote copies, remote signals or barrier semaphores. Data moves between devices by JAX's collectives and lax.ppermute only.
A program may use at most 256 MiB of HBM per device.

```python
import math
import jax
import jax.numpy as jnp
from jax import lax

HEAD_DIM = 128
D = 5120
BLOCKS = 8
TOKENS = 4096
N_HEAD = 4


def pair_fields(key):
    key_query = jax.random.fold_in(key, 11)
    key_key = jax.random.fold_in(key, 12)
    query_field = 2.5 * jnp.clip(jax.random.normal(key_query, (TOKENS, D), jnp.float32), -4.0, 4.0)
    key_field = jnp.clip(jax.random.normal(key_key, (TOKENS, D), jnp.float32), -4.0, 4.0)
    return (query_field, key_field)


def draw_query_vectors(key, part):
    return pair_fields(key)[0].astype(jnp.bfloat16)


def draw_key_vectors(key, part):
    return pair_fields(key)[1].astype(jnp.bfloat16)


def draw_band_table(key, part):
    numbers = jnp.arange(BLOCKS, dtype=jnp.int32)
    distance = jnp.abs(numbers[:, None] - numbers[None, :])
    digits = jnp.zeros((BLOCKS, BLOCKS), jnp.int32)
    for exponent in range(12):
        digits = digits + (jnp.right_shift(distance, exponent) > 0).astype(jnp.int32)
    extra = jax.random.randint(jax.random.fold_in(key, 21), (BLOCKS, BLOCKS), 0, 2, dtype=jnp.int32)
    extra = extra.at[0, BLOCKS - 1].set(1)
    return jnp.where(distance > 0, digits + extra, 0).astype(jnp.int32)


def level_of(rng, shape, pieces, least, high):
    level, own = 1.0, jax.random.fold_in(rng, 6)
    for dim, blocks in pieces:
        steps = jnp.exp(jax.random.uniform(jax.random.fold_in(own, dim), (blocks,), jnp.float32, least / len(pieces), high / len(pieces)))
        level = level * jnp.repeat(steps, shape[dim] // blocks).reshape([-1 if axis == dim else 1 for axis in range(len(shape))])
    return level


def scatter_about(own_key, dims, width, reach, split=(), held_as=jnp.bfloat16):
    values = jax.random.normal(own_key, dims, jnp.float32) * width
    if len(split) > 0:
        values = level_of(own_key, dims, split, -0.22, 0.18) * values
    return jnp.clip(values, min=-reach, max=reach).astype(held_as)


def setup_inputs(seed: int = 0) -> dict:
    keys = jax.random.split(jax.random.key(seed), 6)
    return {
        "query_vectors": draw_query_vectors(jax.random.fold_in(keys[5], 71), 0),
        "key_vectors": draw_key_vectors(jax.random.fold_in(keys[5], 71), 0),
        "value_vectors": scatter_about(keys[2], (TOKENS, D), 2.0, 8.0, ((0, 8), (1, 4))),
        "band_table": draw_band_table(jax.random.fold_in(keys[5], 71), 0),
        "out_weight": scatter_about(keys[4], (D, D), D ** -0.5, 0.078125, ((0, 4),)),
    }


def reference(query_vectors, key_vectors, value_vectors, band_table, out_weight):
    block_count = band_table.shape[0]
    row_count = query_vectors.shape[0] // block_count
    head_count = query_vectors.shape[1] // HEAD_DIM
    score_scale = 1.0 / math.sqrt(HEAD_DIM)
    query_blocks = query_vectors.reshape(block_count, row_count, head_count, HEAD_DIM)
    key_blocks = key_vectors.reshape(block_count, row_count, head_count, HEAD_DIM)
    value_blocks = value_vectors.reshape(block_count, row_count, head_count, HEAD_DIM)
    half_keys = key_blocks[:, ::2]
    half_values = value_blocks[:, ::2]
    row_numbers = jnp.arange(row_count, dtype=jnp.int32)
    half_numbers = row_numbers[::2]
    block_numbers = jnp.arange(block_count, dtype=jnp.int32)

    def scores_of(query_rows, key_rows):
        return jnp.einsum('qhd,khd->qhk', query_rows.astype(jnp.float32), key_rows.astype(jnp.float32)) * score_scale

    def keep_of(numbers, band_value):
        return jnp.remainder(numbers, jnp.left_shift(jnp.int32(1), band_value)) == 0

    def one_block(inputs):
        query_rows, own_keys, own_values, table_row, own_number = inputs
        own_keep = keep_of(row_numbers, table_row[own_number])
        own_scores = jnp.where(own_keep[None, None, :], scores_of(query_rows, own_keys), -1e+30)

        def max_step(running, inputs_far):
            far_keys, block_number = inputs_far
            far_keep = keep_of(half_numbers, table_row[block_number]) & (block_number != own_number)
            far_scores = jnp.where(far_keep[None, None, :], scores_of(query_rows, far_keys), -1e+30)
            return (jnp.maximum(running, lax.optimization_barrier(jnp.max(far_scores, axis=2))), None)
        row_max, _ = lax.scan(max_step, lax.optimization_barrier(jnp.max(own_scores, axis=2)), (half_keys, block_numbers))

        def weigh(scores, kept_mask):
            return jnp.where(kept_mask[None, None, :], jnp.exp(scores - row_max[:, :, None]), 0.0)
        own_weights = weigh(own_scores, own_keep)
        denominator = lax.optimization_barrier(jnp.sum(own_weights, axis=2))
        accum = jnp.einsum('qhk,khd->qhd', own_weights.astype(jnp.bfloat16).astype(jnp.float32), own_values.astype(jnp.float32))

        def sum_step(carry, inputs_far):
            denom_now, accum_now = carry
            far_keys, far_values, block_number = inputs_far
            far_keep = keep_of(half_numbers, table_row[block_number]) & (block_number != own_number)
            far_weights = weigh(scores_of(query_rows, far_keys), far_keep)
            rounded = far_weights.astype(jnp.bfloat16)
            accum_now = accum_now + jnp.einsum('qhk,khd->qhd', rounded.astype(jnp.float32), far_values.astype(jnp.float32))
            denom_now = denom_now + lax.optimization_barrier(jnp.sum(far_weights, axis=2))
            return ((denom_now, accum_now), None)
        (denominator, accum), _ = lax.scan(sum_step, (denominator, accum), (half_keys, half_values, block_numbers))
        result = accum / denominator[:, :, None]
        return result.reshape(row_count, head_count * HEAD_DIM).astype(jnp.bfloat16)
    attention = lax.map(one_block, (query_blocks, key_blocks, value_blocks, band_table, block_numbers))
    attention = attention.reshape(block_count * row_count, head_count * HEAD_DIM)
    group_width = attention.shape[1] // N_HEAD
    total = jnp.zeros((attention.shape[0], out_weight.shape[1]), jnp.float32)
    for group_number in range(N_HEAD):
        low = group_number * group_width
        partial_sum = jnp.dot(attention[:, low:low + group_width], out_weight[low:low + group_width], preferred_element_type=jnp.float32)
        total = total + lax.optimization_barrier(partial_sum.astype(jnp.bfloat16)).astype(jnp.float32)
    return total.astype(jnp.bfloat16)
```

```python
import math

import jax
import jax.numpy as jnp
import numpy as np
from jax import lax
from jax.experimental import pallas as pl
from jax.experimental.pallas import tpu as pltpu
from jax.sharding import PartitionSpec as P

HEAD_DIM = 128
MASKED = -1e30
AXES = ("tm", "head")
F32 = jnp.float32
BF16 = jnp.bfloat16


def prefix_order(row_count):
    rows = np.arange(0, row_count, 2)
    zeros = [(r & -r).bit_length() if r else 64 for r in rows.tolist()]
    return rows[np.argsort([-z for z in zeros], kind="stable")]


def pack_kernel(order_ref, key_ref, value_ref, *out_refs, cuts):
    picks = order_ref.shape[0]
    row_count = key_ref.shape[0]
    column = lax.broadcasted_iota(jnp.int32, (picks, row_count), 1)
    choose = jnp.where(order_ref[...] == column, 1.0, 0.0).astype(BF16)
    for plane, source in enumerate((key_ref, value_ref)):
        picked = jnp.dot(choose, source[...], preferred_element_type=F32).astype(BF16)
        for out_ref, (low, high) in zip(out_refs, cuts):
            out_ref[plane] = picked[low:high]


def pack(key_vectors, value_vectors, order, cuts):
    row_count, width = key_vectors.shape
    tile = 256
    picks = len(order)
    rows = jnp.asarray(order.astype(np.int32)[:, None])
    return pl.pallas_call(
        lambda *refs: pack_kernel(*refs, cuts=cuts),
        grid=(width // tile,),
        in_specs=[
            pl.BlockSpec((picks, 1), lambda j: (0, 0)),
            pl.BlockSpec((row_count, tile), lambda j: (0, j)),
            pl.BlockSpec((row_count, tile), lambda j: (0, j)),
        ],
        out_specs=[
            pl.BlockSpec((2, high - low, tile), lambda j: (0, 0, j)) for low, high in cuts
        ],
        out_shape=[jax.ShapeDtypeStruct((2, high - low, width), BF16) for low, high in cuts],
        name="pack",
        cost_estimate=pl.CostEstimate(
            flops=4 * picks * row_count * width, bytes_accessed=8 * row_count * width, transcendentals=0
        ),
    )(rows, key_vectors, value_vectors)


def attend_kernel(*refs, buffers, own, first, last, row_tile):
    refs = list(refs)
    query_ref = refs.pop(0)
    if own:
        keys = [refs.pop(0)[...]]
        values = [refs.pop(0)[...]]
    else:
        keys, values = ([], [])
    for _ in range(buffers):
        packed = refs.pop(0)
        keys.append(packed[0])
        values.append(packed[1])
    bias = None if own else refs.pop(0)[...]
    if not first:
        state_in, accum_in = (refs.pop(0), refs.pop(0))
    out_refs = refs
    key = keys[0] if len(keys) == 1 else jnp.concatenate(keys, axis=0)
    value = values[0] if len(values) == 1 else jnp.concatenate(values, axis=0)
    factor = math.log2(math.e) / math.sqrt(HEAD_DIM)
    for low in range(0, query_ref.shape[0], row_tile):
        rows = pl.ds(low, row_tile)
        scores = lax.dot_general(
            query_ref[rows, :], key, (((1,), (1,)), ((), ())), preferred_element_type=F32
        )
        scores = scores * factor
        if bias is not None:
            scores = scores + bias
        top = jnp.max(scores, axis=1, keepdims=True)
        if not first:
            top_in = state_in[rows, :][:, :1]
            top = jnp.maximum(top, top_in)
            shrink = jnp.exp2(top_in - top)
        weights = jnp.exp2(scores - top)
        total = jnp.sum(weights, axis=1, keepdims=True)
        accum = jnp.dot(weights.astype(BF16), value, preferred_element_type=F32)
        if not first:
            total = total + shrink * state_in[rows, :][:, 64:65]
            accum = accum + shrink * accum_in[rows, :]
        if last:
            out_refs[0][rows, :] = (accum / total).astype(BF16)
        else:
            lane = lax.broadcasted_iota(jnp.int32, (row_tile, HEAD_DIM), 1)
            out_refs[0][rows, :] = jnp.where(lane < 64, top, total)
            out_refs[1][rows, :] = accum


def attend(query_vectors, own_pair, buffers, bias, carry, last, name):
    row_count, width = query_vectors.shape
    head_count = width // HEAD_DIM
    whole = pl.BlockSpec((row_count, HEAD_DIM), lambda h: (0, h))
    operands, specs = ([query_vectors], [whole])
    own = own_pair is not None
    count = 0
    if own:
        operands += list(own_pair)
        specs += [whole, whole]
        count += row_count
    for buffer in buffers:
        operands.append(buffer)
        specs.append(pl.BlockSpec((2, buffer.shape[1], HEAD_DIM), lambda h: (0, 0, h)))
        count += buffer.shape[1]
    if not own:
        operands.append(bias)
        specs.append(pl.BlockSpec((1, count), lambda h: (0, 0)))
    first = carry is None
    if not first:
        operands += list(carry)
        specs += [whole, whole]
    if last:
        shapes = [jax.ShapeDtypeStruct((row_count, width), BF16)]
    else:
        shapes = [jax.ShapeDtypeStruct((row_count, width), F32)] * 2
    return pl.pallas_call(
        lambda *refs: attend_kernel(
            *refs, buffers=len(buffers), own=own, first=first, last=last, row_tile=256
        ),
        grid=(head_count,),
        in_specs=specs,
        out_specs=[whole] * len(shapes),
        out_shape=shapes,
        name=name,
        cost_estimate=pl.CostEstimate(
            flops=4 * row_count * count * width,
            bytes_accessed=4 * row_count * width,
            transcendentals=row_count * count * head_count,
        ),
    )(*operands)


def project_kernel(place_ref, mine_ref, other_ref, weight_ref, moved_ref, out_ref):
    total = jnp.dot(mine_ref[...], weight_ref[...], preferred_element_type=F32)
    total = total + jnp.dot(other_ref[...], moved_ref[...], preferred_element_type=F32)
    out_ref[...] = total.astype(out_ref.dtype)


def project(place, mine, other, weight, moved, half, out_type, name):
    rows, depth = mine.shape
    width = moved.shape[1]
    tile = 256
    steps = width // tile
    return pl.pallas_call(
        project_kernel,
        grid_spec=pltpu.PrefetchScalarGridSpec(
            num_scalar_prefetch=1,
            grid=(steps,),
            in_specs=[
                pl.BlockSpec((rows, depth), lambda j, place: (0, 0)),
                pl.BlockSpec((rows, depth), lambda j, place: (0, 0)),
                pl.BlockSpec((depth, tile), lambda j, place: (0, place[0] * steps + j)),
                pl.BlockSpec((depth, tile), lambda j, place: (half, j)),
            ],
            out_specs=pl.BlockSpec((rows, tile), lambda j, place: (0, j)),
        ),
        out_shape=jax.ShapeDtypeStruct((rows, width), out_type),
        name=name,
        cost_estimate=pl.CostEstimate(
            flops=4 * rows * depth * width, bytes_accessed=4 * depth * width, transcendentals=0
        ),
    )(place, mine, other, weight, moved)


def per_device(query_vectors, key_vectors, value_vectors, band_table, out_weight):
    row_count, width = query_vectors.shape
    block_count = lax.axis_size("tm")
    group_count = lax.axis_size("head")
    my_block = lax.axis_index("tm")
    my_group = lax.axis_index("head")
    table_row = lax.dynamic_index_in_dim(band_table, my_block, 0, keepdims=False)

    def move(array, block_to, group_to=lambda h: h):
        route = []
        for t in range(block_count):
            for h in range(group_count):
                to = block_to(t)
                if to is not None and 0 <= to < block_count:
                    route.append((t * group_count + h, to * group_count + group_to(h)))
        return lax.ppermute(array, AXES, route)

    def bias_of(pieces):
        blocks = jnp.stack([jnp.asarray(block, jnp.int32) for block, _, _ in pieces])
        number = np.concatenate([np.full(n, i) for i, (_, _, n) in enumerate(pieces)])
        rank = np.concatenate([np.arange(a, a + n) for _, a, n in pieces]).astype(np.int32)
        member = jnp.asarray(number[None, :] == np.arange(len(pieces))[:, None])
        here = jnp.arange(block_count, dtype=jnp.int32)[None, :] == blocks[:, None]
        band = jnp.sum(jnp.where(here, table_row[None, :], 0), axis=1)
        kept = jnp.where(jnp.any(here, axis=1), jnp.right_shift(jnp.int32(row_count), band), 0)
        limit = jnp.sum(jnp.where(member, kept[:, None], 0), axis=0)
        return jnp.where(jnp.asarray(rank) < limit, 0.0, MASKED).astype(F32)[None, :]

    order = prefix_order(row_count)
    near = row_count // 2
    if block_count == 8:
        a, ab = (row_count // 8, row_count // 4)
        even = my_block % 2 == 0
        side = jnp.where(even, 1, -1)
        z = my_block // 2
        sent_bc, sent_a, sent_ab = pack(
            key_vectors, value_vectors, order, [(a, near), (0, a), (0, ab)]
        )
        twin = lambda t: t ^ 1
        far_way = lambda t: t + 2 if t % 2 == 0 else t - 2
        near_way = lambda t: t - 2 if t % 2 == 0 else t + 2
        x_bc = move(sent_bc, twin)
        x_a = move(sent_a, twin)
        z_far = move(sent_ab, far_way)
        z_near = move(sent_ab, near_way)
        z_two = move(sent_ab, lambda t: t ^ 4)
        near_bc = move(x_bc, far_way)
        cross_far = move(z_far, lambda t: t ^ 1 if 0 <= (t - 2 if t % 2 == 0 else t + 2) < 8 else None)
        cross_near = move(
            z_near[:, :a], lambda t: t ^ 1 if 0 <= (t + 2 if t % 2 == 0 else t - 2) < 8 else None
        )
        z_three = move(z_two[:, :a], lambda t: {4: 6, 5: 7, 2: 0, 3: 1}.get(t))
        cross_two = move(z_two, twin)
        cross_three = move(z_three, lambda t: t ^ 1 if t in (0, 1, 6, 7) else None)
        partner = my_block ^ 1
        far_block = my_block - 2 * side
        near_block = my_block + 2 * side
        two = my_block ^ 4
        three = jnp.where((z == 0) | (z == 3), 6 - 2 * z + my_block % 2, -1)
        adjacent = my_block - side
        far_cross = my_block + 3 * side
        two_cross = two ^ 1
        three_cross = jnp.where(three >= 0, three ^ 1, -1)
        stages = [
            [(x_bc, partner, a), (x_a, partner, 0), (z_far, far_block, 0), (z_near, near_block, 0)],
            [
                (z_two, two, 0),
                (near_bc, adjacent, a),
                (cross_near, adjacent, 0),
                (cross_far, far_cross, 0),
            ],
            [(cross_two, two_cross, 0), (z_three, three, 0), (cross_three, three_cross, 0)],
        ]
    else:
        (packed,) = pack(key_vectors, value_vectors, order, [(0, near)])
        received, blocks = ([], [])
        for distance in range(1, block_count):
            rows = row_count >> distance.bit_length()
            for sign in (1, -1):
                received.append(move(packed[:, :rows], lambda t: t + sign * distance))
                blocks.append((my_block - sign * distance, 0, rows))
        joined = jnp.concatenate(received, axis=1)
        stages = [[(joined, blocks)]]

    core = lambda h: h ^ 1
    mine = my_group % 2
    level = my_group // 2
    out_width = out_weight.shape[1] // group_count
    columns = lambda number: lax.dynamic_slice_in_dim(out_weight, number * out_width, out_width, 1)
    theirs = jnp.concatenate(
        [columns(2 * (1 - level) + 1 - mine), columns(2 * level + 1 - mine)], axis=0
    )
    moved = move(theirs, lambda t: t, core)

    carry = attend(query_vectors, (key_vectors, value_vectors), [], None, None, False, "own")
    for number, stage in enumerate(stages):
        last = number == len(stages) - 1
        if block_count == 8:
            pieces = [(block, low, buffer.shape[1]) for buffer, block, low in stage]
            buffers = [buffer for buffer, _, _ in stage]
        else:
            buffers = [stage[0][0]]
            pieces = stage[0][1]
        carry = attend(
            query_vectors, None, buffers, bias_of(pieces), carry, last, f"stage{number}"
        )
    attention = carry[0]
    other = move(attention, lambda t: t, core)
    away = jnp.reshape(2 * (1 - level) + mine, (1,))
    home = jnp.reshape(2 * level + mine, (1,))
    sent = project(away, attention, other, out_weight, moved, 0, BF16, "away")
    arrived = move(sent, lambda t: t, lambda h: h ^ 2)
    kept = project(home, attention, other, out_weight, moved, 1, F32, "home")
    return (kept + arrived.astype(F32)).astype(BF16)


def solution(mesh):
    in_specs = (P("tm", "head"), P("tm", "head"), P("tm", "head"), P(), P("head", None))
    out_specs = P("tm", "head")
    return jax.shard_map(
        per_device, mesh=mesh, in_specs=in_specs, out_specs=out_specs, check_vma=False
    )
```

```python
import math

import jax
import jax.numpy as jnp
import numpy as np
from jax import lax
from jax.experimental import pallas as pl
from jax.experimental.pallas import tpu as pltpu
from jax.sharding import PartitionSpec as P

HEAD_DIM = 128
MASKED = -1e30
AXES = ("tm", "head")
F32 = jnp.float32
BF16 = jnp.bfloat16


def prefix_order(row_count):
    rows = np.arange(0, row_count, 2)
    zeros = [(r & -r).bit_length() if r else 64 for r in rows.tolist()]
    return rows[np.argsort([-z for z in zeros], kind="stable")]


def pack_kernel(order_ref, key_ref, value_ref, *out_refs, cuts):
    picks = order_ref.shape[0]
    row_count = key_ref.shape[0]
    column = lax.broadcasted_iota(jnp.int32, (picks, row_count), 1)
    choose = jnp.where(order_ref[...] == column, 1.0, 0.0).astype(BF16)
    for plane, source in enumerate((key_ref, value_ref)):
        picked = jnp.dot(choose, source[...], preferred_element_type=F32).astype(BF16)
        for out_ref, (low, high) in zip(out_refs, cuts):
            out_ref[plane] = picked[low:high]


def pack(key_vectors, value_vectors, order, cuts):
    row_count, width = key_vectors.shape
    tile = width // 2
    picks = len(order)
    rows = jnp.asarray(order.astype(np.int32)[:, None])
    return pl.pallas_call(
        lambda *refs: pack_kernel(*refs, cuts=cuts),
        grid=(width // tile,),
        in_specs=[
            pl.BlockSpec((picks, 1), lambda j: (0, 0)),
            pl.BlockSpec((row_count, tile), lambda j: (0, j)),
            pl.BlockSpec((row_count, tile), lambda j: (0, j)),
        ],
        out_specs=[
            pl.BlockSpec((2, high - low, tile), lambda j: (0, 0, j)) for low, high in cuts
        ],
        out_shape=[jax.ShapeDtypeStruct((2, high - low, width), BF16) for low, high in cuts],
        name="pack",
        compiler_params=pltpu.CompilerParams(vmem_limit_bytes=48 << 20),
        cost_estimate=pl.CostEstimate(
            flops=4 * picks * row_count * width, bytes_accessed=8 * row_count * width, transcendentals=0
        ),
    )(rows, key_vectors, value_vectors)


def attend_kernel(*refs, buffers, own, first, last, heads):
    refs = list(refs)
    query_ref = refs.pop(0)
    own_refs = [refs.pop(0), refs.pop(0)] if own else None
    packed_refs = [refs.pop(0) for _ in range(buffers)]
    bias_ref = refs.pop(0)
    state_in, accum_in = (None, None) if first else (refs.pop(0), refs.pop(0))
    query_count = query_ref.shape[0]
    factor = math.log2(math.e) / math.sqrt(HEAD_DIM)
    bias = jnp.concatenate([bias_ref[...]] * (query_count // HEAD_DIM), axis=1)
    for head in range(heads):
        span = slice(head * HEAD_DIM, (head + 1) * HEAD_DIM)
        keys = [ref[0, :, span] for ref in packed_refs]
        values = [ref[1, :, span] for ref in packed_refs]
        key = keys[0] if len(keys) == 1 else jnp.concatenate(keys, axis=0)
        value = values[0] if len(values) == 1 else jnp.concatenate(values, axis=0)
        query = query_ref[:, span]
        by_last = (((1,), (1,)), ((), ()))
        scores = lax.dot_general(key, query, by_last, preferred_element_type=F32) + bias
        top = jnp.max(scores, axis=0, keepdims=True)
        if own:
            own_scores = lax.dot_general(
                own_refs[0][:, span], query, by_last, preferred_element_type=F32
            )
            top = jnp.maximum(top, jnp.max(own_scores, axis=0, keepdims=True))
        if not first:
            top_in = state_in[head, 0:1, :]
            top = jnp.maximum(top, top_in)
            shrink = jnp.exp2((top_in - top) * factor)
        level = top * factor
        weights = jnp.exp2(scores * factor - level)
        total = jnp.sum(weights, axis=0, keepdims=True)
        accum = jnp.dot(value.T, weights.astype(BF16), preferred_element_type=F32)
        if own:
            own_weights = jnp.exp2(own_scores * factor - level)
            total = total + jnp.sum(own_weights, axis=0, keepdims=True)
            accum = accum + jnp.dot(
                own_refs[1][:, span].T, own_weights.astype(BF16), preferred_element_type=F32
            )
        if not first:
            total = total + shrink * state_in[head, 1:2, :]
            accum = accum + shrink * accum_in[head]
        if last:
            refs[0][:, span] = (accum / total).T.astype(BF16)
        else:
            refs[0][head, 0:1, :] = top
            refs[0][head, 1:2, :] = total
            refs[1][head] = accum


def attend(query_vectors, own_pair, buffers, bias, carry, last, heads, name):
    row_count, width = query_vectors.shape
    head_count = width // HEAD_DIM
    span = heads * HEAD_DIM
    whole = pl.BlockSpec((row_count, span), lambda h: (0, h))
    state = pl.BlockSpec((heads, 8, row_count), lambda h: (h, 0, 0))
    accum = pl.BlockSpec((heads, HEAD_DIM, row_count), lambda h: (h, 0, 0))
    operands, specs = ([query_vectors], [whole])
    own = own_pair is not None
    count = bias.shape[0]
    if own:
        operands += list(own_pair)
        specs += [whole, whole]
    for buffer in buffers:
        operands.append(buffer)
        specs.append(pl.BlockSpec((2, buffer.shape[1], span), lambda h: (0, 0, h)))
    operands.append(bias)
    specs.append(pl.BlockSpec((count, HEAD_DIM), lambda h: (0, 0)))
    first = carry is None
    if not first:
        operands += list(carry)
        specs += [state, accum]
    if last:
        shapes = [jax.ShapeDtypeStruct((row_count, width), BF16)]
        out_specs = [whole]
    else:
        shapes = [
            jax.ShapeDtypeStruct((head_count, 8, row_count), F32),
            jax.ShapeDtypeStruct((head_count, HEAD_DIM, row_count), F32),
        ]
        out_specs = [state, accum]
    total = count + (row_count if own else 0)
    return pl.pallas_call(
        lambda *refs: attend_kernel(
            *refs, buffers=len(buffers), own=own, first=first, last=last, heads=heads
        ),
        grid=(head_count // heads,),
        in_specs=specs,
        out_specs=out_specs,
        out_shape=shapes,
        name=name,
        compiler_params=pltpu.CompilerParams(vmem_limit_bytes=48 << 20),
        cost_estimate=pl.CostEstimate(
            flops=4 * row_count * total * width,
            bytes_accessed=8 * row_count * width,
            transcendentals=row_count * total * head_count,
        ),
    )(*operands)


def per_device(query_vectors, key_vectors, value_vectors, band_table, out_weight):
    row_count, width = query_vectors.shape
    block_count = lax.axis_size("tm")
    group_count = lax.axis_size("head")
    my_block = lax.axis_index("tm")
    my_group = lax.axis_index("head")
    table_row = lax.dynamic_index_in_dim(band_table, my_block, 0, keepdims=False)

    def move(array, block_to, group_to=lambda h: h):
        route = []
        for t in range(block_count):
            for h in range(group_count):
                to = block_to(t)
                if to is not None and 0 <= to < block_count:
                    route.append((t * group_count + h, to * group_count + group_to(h)))
        return lax.ppermute(array, AXES, route)

    def bias_of(pieces):
        blocks = jnp.stack([jnp.asarray(block, jnp.int32) for block, _, _ in pieces])
        number = np.concatenate([np.full(n, i) for i, (_, _, n) in enumerate(pieces)])
        rank = np.concatenate([np.arange(a, a + n) for _, a, n in pieces]).astype(np.int32)
        member = jnp.asarray(number[None, :] == np.arange(len(pieces))[:, None])
        here = jnp.arange(block_count, dtype=jnp.int32)[None, :] == blocks[:, None]
        band = jnp.sum(jnp.where(here, table_row[None, :], 0), axis=1)
        kept = jnp.where(jnp.any(here, axis=1), jnp.right_shift(jnp.int32(row_count), band), 0)
        limit = jnp.sum(jnp.where(member, kept[:, None], 0), axis=0)
        bias = jnp.where(jnp.asarray(rank) < limit, 0.0, MASKED).astype(F32)
        return jnp.broadcast_to(bias[:, None], (rank.size, HEAD_DIM))

    order = prefix_order(row_count)
    near = row_count // 2
    if block_count == 8:
        a, ab = (row_count // 8, row_count // 4)
        side = jnp.where(my_block % 2 == 0, 1, -1)
        far_way = lambda t: t + 2 if t % 2 == 0 else t - 2
        near_way = lambda t: t - 2 if t % 2 == 0 else t + 2
        partner = my_block ^ 1
        far_block, near_block = (my_block - 2 * side, my_block + 2 * side)
        two, opposite = (my_block ^ 4, my_block ^ 6)
        adjacent, far_cross = (my_block - side, my_block + 3 * side)
        at_end = (my_block < 2) | (my_block >= block_count - 2)
        sent, sent_ab, sent_a = pack(key_vectors, value_vectors, order, [(0, near), (0, ab), (0, a)])
        x_rows = move(sent, lambda t: t ^ 1)
        z_far = move(sent_ab, far_way)
        z_near = move(sent_ab, near_way)
        z_two = move(sent_a, lambda t: t ^ 4)
        z_three = move(sent_a, lambda t: t ^ 6 if t in (0, 1, 6, 7) else None)
        x_rows, z_far, z_near, z_two, z_three, out_weight = lax.optimization_barrier(
            (x_rows, z_far, z_near, z_two, z_three, out_weight)
        )
        behind = x_rows[:, a:]
        has_far = (far_block >= 0) & (far_block < block_count)
        has_near = (near_block >= 0) & (near_block < block_count)
        slot_far = jnp.where(has_far, z_far[:, :a], z_three)
        slot_near = jnp.where(has_near, z_near[:, :a], z_three)
        relayed = jnp.concatenate([slot_far, z_far[:, a:], slot_near, z_two], axis=1)
        near_bc = move(behind, far_way)
        crossed = move(relayed, lambda t: t ^ 1)
        none = jnp.int32(-1)
        three = jnp.where(at_end, opposite, none)
        three_cross = jnp.where(at_end, opposite ^ 1, none)
        has_far_cross = (far_cross >= 0) & (far_cross < block_count)
        has_adjacent = (adjacent >= 0) & (adjacent < block_count)
        stages = [
            (
                [x_rows, z_far, z_near, z_two, z_three],
                [
                    (partner, 0, near),
                    (far_block, 0, ab),
                    (near_block, 0, ab),
                    (two, 0, a),
                    (three, 0, a),
                ],
            ),
            (
                [near_bc, crossed],
                [
                    (adjacent, a, near - a),
                    (jnp.where(has_far_cross, far_cross, three_cross), 0, a),
                    (far_cross, a, ab - a),
                    (jnp.where(has_adjacent, adjacent, three_cross), 0, a),
                    (two ^ 1, 0, a),
                    (my_block - 3 * side, a, ab - a),
                ],
            ),
        ]
    else:
        (packed,) = pack(key_vectors, value_vectors, order, [(0, near)])
        received, blocks = ([], [])
        for distance in range(1, block_count):
            rows = row_count >> distance.bit_length()
            for sign in (1, -1):
                received.append(move(packed[:, :rows], lambda t: t + sign * distance))
                blocks.append((my_block - sign * distance, 0, rows))
        stages = [
            ([jnp.concatenate(received[:2], axis=1)], blocks[:2]),
            ([jnp.concatenate(received[2:], axis=1)], blocks[2:]),
        ]

    own_pair = (key_vectors, value_vectors)
    buffers, pieces = stages[0]
    bias = bias_of(pieces)
    carry = attend(query_vectors, own_pair, buffers, bias, None, False, 2, "first")
    buffers, pieces = stages[1]
    if block_count == 8:
        near_bc, crossed = buffers
        near_bc, state = lax.optimization_barrier((near_bc, carry[0]))
        carry = (state, carry[1])
        buffers = [near_bc, crossed, move(near_bc[:, :a], far_way)]

    core = lambda h: h ^ 1
    same = lambda t: t
    mine = my_group % 2
    level = my_group // 2
    out_width = out_weight.shape[1] // group_count
    columns = lambda number: lax.dynamic_slice_in_dim(out_weight, number * out_width, out_width, 1)
    away, home = (2 * (1 - level) + mine, 2 * level + mine)
    moved = move(out_weight, same, core)

    carry = attend(query_vectors, None, buffers, bias_of(pieces), carry, True, 2, "second")
    attention = carry[0]
    other = move(attention, same, core)

    def project(number, low, span):
        start = number * out_width + low
        own_weight = lax.dynamic_slice_in_dim(out_weight, start, span, 1)
        other_weight = lax.dynamic_slice_in_dim(moved, start, span, 1)
        total = jnp.dot(attention, own_weight, preferred_element_type=F32)
        return total + jnp.dot(other, other_weight, preferred_element_type=F32)

    half = out_width // 2
    arrived = [
        move(project(away, low, half).astype(BF16), same, lambda h: h ^ 2) for low in (0, half)
    ]
    kept = project(home, 0, out_width)
    return (kept + jnp.concatenate(arrived, axis=1).astype(F32)).astype(BF16)


def solution(mesh):
    in_specs = (P("tm", "head"), P("tm", "head"), P("tm", "head"), P(), P("head", None))
    out_specs = P("tm", "head")
    return jax.shard_map(
        per_device, mesh=mesh, in_specs=in_specs, out_specs=out_specs, check_vma=False
    )
```

```python
import math

import jax
import jax.numpy as jnp
import numpy as np
from jax import lax
from jax.experimental import pallas as pl
from jax.experimental.pallas import tpu as pltpu
from jax.sharding import PartitionSpec as P

HEAD_DIM = 128
MASKED = -1e30
AXES = ("tm", "head")
F32 = jnp.float32
BF16 = jnp.bfloat16


def pack_kernel(key_ref, value_ref, *out_refs, cuts):
    row_count = key_ref.shape[0]
    picks = row_count // 2
    rank = lax.broadcasted_iota(jnp.int32, (picks, 1), 0)
    place = jnp.zeros_like(rank)
    step = 1
    while step < picks:
        stride = row_count // (2 * step)
        place = jnp.where(rank >= step, (2 * (rank - step) + 1) * stride, place)
        step *= 2
    column = lax.broadcasted_iota(jnp.int32, (picks, row_count), 1)
    choose = jnp.where(place == column, 1.0, 0.0).astype(BF16)
    for plane, source in enumerate((key_ref, value_ref)):
        picked = jnp.dot(choose, source[...], preferred_element_type=F32).astype(BF16)
        for out_ref, (low, high) in zip(out_refs, cuts):
            out_ref[plane] = picked[low:high]


def pack(key_vectors, value_vectors, cuts):
    row_count, width = key_vectors.shape
    tile = width // 2
    return pl.pallas_call(
        lambda *refs: pack_kernel(*refs, cuts=cuts),
        grid=(width // tile,),
        in_specs=[pl.BlockSpec((row_count, tile), lambda j: (0, j))] * 2,
        out_specs=[
            pl.BlockSpec((2, high - low, tile), lambda j: (0, 0, j)) for low, high in cuts
        ],
        out_shape=[jax.ShapeDtypeStruct((2, high - low, width), BF16) for low, high in cuts],
        name="pack",
        compiler_params=pltpu.CompilerParams(vmem_limit_bytes=48 << 20),
        cost_estimate=pl.CostEstimate(
            flops=2 * row_count * row_count * width,
            bytes_accessed=8 * row_count * width,
            transcendentals=0,
        ),
    )(key_vectors, value_vectors)


def attend_kernel(*refs, buffers, own, first, last, heads):
    refs = list(refs)
    query_ref = refs.pop(0)
    own_refs = [refs.pop(0), refs.pop(0)] if own else None
    packed_refs = [refs.pop(0) for _ in range(buffers)]
    bias_ref = refs.pop(0) if buffers else None
    state_in, accum_in = (None, None) if first else (refs.pop(0), refs.pop(0))
    query_count = query_ref.shape[0]
    factor = math.log2(math.e) / math.sqrt(HEAD_DIM)
    if buffers:
        bias = jnp.concatenate([bias_ref[...]] * (query_count // HEAD_DIM), axis=1)
    for head in range(heads):
        span = slice(head * HEAD_DIM, (head + 1) * HEAD_DIM)
        if own:
            key, value = (own_refs[0][:, span], own_refs[1][:, span])
        else:
            key = jnp.concatenate([ref[0, :, span] for ref in packed_refs], axis=0)
            value = jnp.concatenate([ref[1, :, span] for ref in packed_refs], axis=0)
        scores = lax.dot_general(
            key, query_ref[:, span], (((1,), (1,)), ((), ())), preferred_element_type=F32
        )
        if buffers:
            scores = scores + bias
        top = jnp.max(scores, axis=0, keepdims=True)
        if not first:
            top_in = state_in[head, 0:1, :]
            top = jnp.maximum(top, top_in)
            shrink = jnp.exp2((top_in - top) * factor)
        level = top * factor
        weights = jnp.exp2(scores * factor - level)
        total = jnp.sum(weights, axis=0, keepdims=True)
        accum = jnp.dot(value.T, weights.astype(BF16), preferred_element_type=F32)
        if not first:
            total = total + shrink * state_in[head, 1:2, :]
            accum = accum + shrink * accum_in[head]
        if last:
            refs[0][:, span] = (accum / total).T.astype(BF16)
        else:
            refs[0][head, 0:1, :] = top
            refs[0][head, 1:2, :] = total
            refs[1][head] = accum


def attend(query_vectors, own_pair, buffers, bias, carry, last, low, high, name):
    row_count = query_vectors.shape[0]
    heads = 5 if (high - low) % 5 == 0 else 1
    span = heads * HEAD_DIM
    skip = low // heads
    assert low % heads == 0
    whole = pl.BlockSpec((row_count, span), lambda h: (0, h + skip))
    state = pl.BlockSpec((heads, 8, row_count), lambda h: (h, 0, 0))
    accum = pl.BlockSpec((heads, HEAD_DIM, row_count), lambda h: (h, 0, 0))
    state_in = pl.BlockSpec((heads, 8, row_count), lambda h: (h + skip, 0, 0))
    accum_in = pl.BlockSpec((heads, HEAD_DIM, row_count), lambda h: (h + skip, 0, 0))
    operands, specs = ([query_vectors], [whole])
    own = own_pair is not None
    count = row_count if own else bias.shape[0]
    if own:
        operands += list(own_pair)
        specs += [whole, whole]
    for buffer in buffers:
        operands.append(buffer)
        specs.append(pl.BlockSpec((2, buffer.shape[1], span), lambda h: (0, 0, h + skip)))
    if buffers:
        operands.append(bias)
        specs.append(pl.BlockSpec((count, HEAD_DIM), lambda h: (0, 0)))
    first = carry is None
    if not first:
        operands += list(carry)
        specs += [state_in, accum_in]
    width = (high - low) * HEAD_DIM
    if last:
        shapes = [jax.ShapeDtypeStruct((row_count, width), BF16)]
        out_specs = [pl.BlockSpec((row_count, span), lambda h: (0, h))]
    else:
        shapes = [
            jax.ShapeDtypeStruct((high - low, 8, row_count), F32),
            jax.ShapeDtypeStruct((high - low, HEAD_DIM, row_count), F32),
        ]
        out_specs = [state, accum]
    return pl.pallas_call(
        lambda *refs: attend_kernel(
            *refs, buffers=len(buffers), own=own, first=first, last=last, heads=heads
        ),
        grid=((high - low) // heads,),
        in_specs=specs,
        out_specs=out_specs,
        out_shape=shapes,
        name=name,
        compiler_params=pltpu.CompilerParams(vmem_limit_bytes=48 << 20),
        cost_estimate=pl.CostEstimate(
            flops=4 * row_count * count * width,
            bytes_accessed=8 * row_count * width,
            transcendentals=row_count * count * (high - low),
        ),
    )(*operands)


def per_device(query_vectors, key_vectors, value_vectors, band_table, out_weight):
    row_count, width = query_vectors.shape
    block_count = lax.axis_size("tm")
    group_count = lax.axis_size("head")
    my_block = lax.axis_index("tm")
    my_group = lax.axis_index("head")
    table_row = lax.dynamic_index_in_dim(band_table, my_block, 0, keepdims=False)

    def move(array, block_to, group_to=lambda h: h):
        route = []
        for t in range(block_count):
            for h in range(group_count):
                to = block_to(t)
                if to is not None and 0 <= to < block_count:
                    route.append((t * group_count + h, to * group_count + group_to(h)))
        return lax.ppermute(array, AXES, route)

    def bias_of(pieces):
        blocks = jnp.stack([jnp.asarray(block, jnp.int32) for block, _, _ in pieces])
        number = np.concatenate([np.full(n, i) for i, (_, _, n) in enumerate(pieces)])
        rank = np.concatenate([np.arange(a, a + n) for _, a, n in pieces]).astype(np.int32)
        member = jnp.asarray(number[None, :] == np.arange(len(pieces))[:, None])
        here = jnp.arange(block_count, dtype=jnp.int32)[None, :] == blocks[:, None]
        band = jnp.sum(jnp.where(here, table_row[None, :], 0), axis=1)
        kept = jnp.where(jnp.any(here, axis=1), jnp.right_shift(jnp.int32(row_count), band), 0)
        limit = jnp.sum(jnp.where(member, kept[:, None], 0), axis=0)
        bias = jnp.where(jnp.asarray(rank) < limit, 0.0, MASKED).astype(F32)
        return jnp.broadcast_to(bias[:, None], (rank.size, HEAD_DIM))

    def within(block):
        return (block >= 0) & (block < block_count)

    head_count = width // HEAD_DIM
    core = lambda h: h ^ 1
    same = lambda t: t
    mine = my_group % 2
    level = my_group // 2
    out_width = out_weight.shape[1] // group_count
    away, home = (2 * (1 - level) + mine, 2 * level + mine)
    moved = move(out_weight, same, core)
    near = row_count // 2
    own_pair = (key_vectors, value_vectors)

    def further(buffers, pieces, carry, name):
        return attend(
            query_vectors, None, buffers, bias_of(pieces), carry, False, 0, head_count, name
        )

    if block_count == 8:
        a, ab = (row_count // 8, row_count // 4)
        side = jnp.where(my_block % 2 == 0, 1, -1)
        far_way = lambda t: t + 2 if t % 2 == 0 else t - 2
        near_way = lambda t: t - 2 if t % 2 == 0 else t + 2
        partner, two, opposite = (my_block ^ 1, my_block ^ 4, my_block ^ 6)
        far_block, near_block = (my_block - 2 * side, my_block + 2 * side)
        adjacent, far_cross = (my_block - side, my_block + 3 * side)
        at_end = (my_block < 2) | (my_block >= block_count - 2)
        none = jnp.int32(-1)
        three = jnp.where(at_end, opposite, none)

        sent, sent_ab, sent_a = pack(key_vectors, value_vectors, [(0, near), (0, ab), (0, a)])
        x_rows = move(sent, lambda t: t ^ 1)
        z_far = move(sent_ab, far_way)
        z_near = move(sent_ab, near_way)
        z_two = move(sent_a, lambda t: t ^ 4)
        carry = attend(query_vectors, own_pair, [], None, None, False, 0, head_count, "own")
        x_rows, z_far, z_near, state = lax.optimization_barrier((x_rows, z_far, z_near, carry[0]))
        carry = (state, carry[1])
        near_b = move(x_rows[:, a:ab], far_way)
        near_c = move(x_rows[:, ab:], far_way)
        slot_far = jnp.where(within(far_block), z_far[:, :a], z_two)
        slot_near = jnp.where(within(near_block), z_near[:, :a], z_two)
        crossed = move(
            jnp.concatenate([slot_far, z_far[:, a:], slot_near], axis=1), lambda t: t ^ 1
        )
        z_three = move(z_two, lambda t: {4: 6, 5: 7, 2: 0, 3: 1}.get(t))
        carry = further(
            [x_rows, z_far, z_near, z_two],
            [(partner, 0, near), (far_block, 0, ab), (near_block, 0, ab), (two, 0, a)],
            carry,
            "first",
        )
        near_b, z_three, state, out_weight, moved = lax.optimization_barrier(
            (near_b, z_three, carry[0], out_weight, moved)
        )
        carry = (state, carry[1])
        cross_last = move(jnp.where(at_end, z_three, z_two), lambda t: t ^ 1)
        chain_b = move(near_b, far_way)
        carry = further(
            [near_b, near_c, z_three],
            [(adjacent, a, ab - a), (adjacent, ab, near - ab), (three, 0, a)],
            carry,
            "middle",
        )
        buffers = [crossed, cross_last, chain_b]
        pieces = [
            (jnp.where(within(far_cross), far_cross, two ^ 1), 0, a),
            (far_cross, a, ab - a),
            (jnp.where(within(adjacent), adjacent, two ^ 1), 0, a),
            (jnp.where(at_end, opposite ^ 1, two ^ 1), 0, a),
            (my_block - 3 * side, a, ab - a),
        ]
    else:
        (packed,) = pack(key_vectors, value_vectors, [(0, near)])
        received, pieces = ([], [])
        for distance in range(1, block_count):
            rows = row_count >> distance.bit_length()
            for sign in (1, -1):
                received.append(move(packed[:, :rows], lambda t: t + sign * distance))
                pieces.append((my_block - sign * distance, 0, rows))
        carry = attend(query_vectors, own_pair, [], None, None, False, 0, head_count, "own")
        carry = further([jnp.concatenate(received[:2], axis=1)], pieces[:2], carry, "first")
        buffers, pieces = ([jnp.concatenate(received[2:], axis=1)], pieces[2:])

    def block_of(weight, number):
        return lax.dynamic_slice_in_dim(weight, number * out_width, out_width, 1)

    weights = lax.optimization_barrier(
        [block_of(weight, number) for weight in (out_weight, moved) for number in (away, home)]
    )
    bias = bias_of(pieces)
    cut = head_count // 2
    parts = []
    for low, high in ((0, cut), (cut, head_count)):
        (part,) = attend(
            query_vectors, None, buffers, bias, carry, True, low, high, f"last{low}"
        )
        parts.append((part, move(part, same, core), low * HEAD_DIM, high * HEAD_DIM))

    def project(index, first, last):
        total = 0.0
        for part, other, low, high in parts:
            total = total + jnp.dot(
                part, weights[index][low:high, first:last], preferred_element_type=F32
            )
            total = total + jnp.dot(
                other, weights[index + 2][low:high, first:last], preferred_element_type=F32
            )
        return total

    half = out_width // 2
    arrived = [
        move(project(0, first, first + half).astype(BF16), same, lambda h: h ^ 2)
        for first in (0, half)
    ]
    kept, arrived[0] = lax.optimization_barrier((project(1, 0, out_width), arrived[0]))
    return (kept + jnp.concatenate(arrived, axis=1).astype(F32)).astype(BF16)


def solution(mesh):
    in_specs = (P("tm", "head"), P("tm", "head"), P("tm", "head"), P(), P("head", None))
    out_specs = P("tm", "head")
    return jax.shard_map(
        per_device, mesh=mesh, in_specs=in_specs, out_specs=out_specs, check_vma=False
    )
```

```python
import math

import jax
import jax.numpy as jnp
import numpy as np
from jax import lax
from jax.experimental import pallas as pl
from jax.experimental.pallas import tpu as pltpu
from jax.sharding import PartitionSpec as P

HEAD_DIM = 128
MASKED = -1e30
AXES = ("tm", "head")
F32 = jnp.float32
BF16 = jnp.bfloat16


def pack_kernel(key_ref, value_ref, *out_refs, cuts):
    row_count = key_ref.shape[0]
    picks = row_count // 2
    rank = lax.broadcasted_iota(jnp.int32, (picks, 1), 0)
    place = jnp.zeros_like(rank)
    step = 1
    while step < picks:
        stride = row_count // (2 * step)
        place = jnp.where(rank >= step, (2 * (rank - step) + 1) * stride, place)
        step *= 2
    column = lax.broadcasted_iota(jnp.int32, (picks, row_count), 1)
    choose = jnp.where(place == column, 1.0, 0.0).astype(BF16)
    for plane, source in enumerate((key_ref, value_ref)):
        picked = jnp.dot(choose, source[...], preferred_element_type=F32).astype(BF16)
        for out_ref, (low, high) in zip(out_refs, cuts):
            out_ref[plane] = picked[low:high]


def pack(key_vectors, value_vectors, cuts):
    row_count, width = key_vectors.shape
    tile = width // 2
    return pl.pallas_call(
        lambda *refs: pack_kernel(*refs, cuts=cuts),
        grid=(width // tile,),
        in_specs=[pl.BlockSpec((row_count, tile), lambda j: (0, j))] * 2,
        out_specs=[
            pl.BlockSpec((2, high - low, tile), lambda j: (0, 0, j)) for low, high in cuts
        ],
        out_shape=[jax.ShapeDtypeStruct((2, high - low, width), BF16) for low, high in cuts],
        name="pack",
        compiler_params=pltpu.CompilerParams(vmem_limit_bytes=48 << 20),
        cost_estimate=pl.CostEstimate(
            flops=2 * row_count * row_count * width,
            bytes_accessed=8 * row_count * width,
            transcendentals=0,
        ),
    )(key_vectors, value_vectors)


def gather_kernel(flag_ref, far_ref, near_ref, two_ref, out_ref):
    a = two_ref.shape[1]
    ab = far_ref.shape[1]
    far_here, near_here = (flag_ref[0] != 0, flag_ref[1] != 0)
    for plane in range(2):
        two = two_ref[plane]
        out_ref[plane, :a] = jnp.where(far_here, far_ref[plane, :a], two)
        out_ref[plane, a:ab] = far_ref[plane, a:]
        out_ref[plane, ab:] = jnp.where(near_here, near_ref[plane, :a], two)


def gather(flags, far, near, two):
    rows = far.shape[1] + two.shape[1]
    width = two.shape[2]
    tile = width // 2
    spec = lambda count: pl.BlockSpec((2, count, tile), lambda j, flags: (0, 0, j))
    return pl.pallas_call(
        gather_kernel,
        grid_spec=pltpu.PrefetchScalarGridSpec(
            num_scalar_prefetch=1,
            grid=(width // tile,),
            in_specs=[spec(far.shape[1]), spec(near.shape[1]), spec(two.shape[1])],
            out_specs=spec(rows),
        ),
        out_shape=jax.ShapeDtypeStruct((2, rows, width), BF16),
        name="gather",
        cost_estimate=pl.CostEstimate(
            flops=0, bytes_accessed=8 * rows * width, transcendentals=0
        ),
    )(flags, far, near, two)


def attend_kernel(*refs, buffers, own, first, last, heads):
    refs = list(refs)
    query_ref = refs.pop(0)
    own_refs = [refs.pop(0), refs.pop(0)] if own else None
    packed_refs = [refs.pop(0) for _ in range(buffers)]
    bias_ref = refs.pop(0) if buffers else None
    state_in, accum_in = (None, None) if first else (refs.pop(0), refs.pop(0))
    query_count = query_ref.shape[0]
    factor = math.log2(math.e) / math.sqrt(HEAD_DIM)
    if buffers:
        bias = jnp.concatenate([bias_ref[...]] * (query_count // HEAD_DIM), axis=1)
    for head in range(heads):
        span = slice(head * HEAD_DIM, (head + 1) * HEAD_DIM)
        if own:
            key, value = (own_refs[0][:, span], own_refs[1][:, span])
        else:
            key = jnp.concatenate([ref[0, :, span] for ref in packed_refs], axis=0)
            value = jnp.concatenate([ref[1, :, span] for ref in packed_refs], axis=0)
        scores = lax.dot_general(
            key, query_ref[:, span], (((1,), (1,)), ((), ())), preferred_element_type=F32
        )
        if buffers:
            scores = scores + bias
        top = jnp.max(scores, axis=0, keepdims=True)
        if not first:
            top_in = state_in[head, 0:1, :]
            top = jnp.maximum(top, top_in)
            shrink = jnp.exp2((top_in - top) * factor)
        level = top * factor
        weights = jnp.exp2(scores * factor - level)
        total = jnp.sum(weights, axis=0, keepdims=True)
        accum = jnp.dot(value.T, weights.astype(BF16), preferred_element_type=F32)
        if not first:
            total = total + shrink * state_in[head, 1:2, :]
            accum = accum + shrink * accum_in[head]
        if last:
            refs[0][:, span] = (accum / total).T.astype(BF16)
        else:
            refs[0][head, 0:1, :] = top
            refs[0][head, 1:2, :] = total
            refs[1][head] = accum


def attend(query_vectors, own_pair, buffers, bias, carry, last, low, high, name):
    row_count = query_vectors.shape[0]
    heads = 5 if (high - low) % 5 == 0 else 1
    span = heads * HEAD_DIM
    skip = low // heads
    assert low % heads == 0
    whole = pl.BlockSpec((row_count, span), lambda h: (0, h + skip))
    state = pl.BlockSpec((heads, 8, row_count), lambda h: (h, 0, 0))
    accum = pl.BlockSpec((heads, HEAD_DIM, row_count), lambda h: (h, 0, 0))
    state_in = pl.BlockSpec((heads, 8, row_count), lambda h: (h + skip, 0, 0))
    accum_in = pl.BlockSpec((heads, HEAD_DIM, row_count), lambda h: (h + skip, 0, 0))
    operands, specs = ([query_vectors], [whole])
    own = own_pair is not None
    count = row_count if own else bias.shape[0]
    if own:
        operands += list(own_pair)
        specs += [whole, whole]
    for buffer in buffers:
        operands.append(buffer)
        specs.append(pl.BlockSpec((2, buffer.shape[1], span), lambda h: (0, 0, h + skip)))
    if buffers:
        operands.append(bias)
        specs.append(pl.BlockSpec((count, HEAD_DIM), lambda h: (0, 0)))
    first = carry is None
    if not first:
        operands += list(carry)
        specs += [state_in, accum_in]
    width = (high - low) * HEAD_DIM
    if last:
        shapes = [jax.ShapeDtypeStruct((row_count, width), BF16)]
        out_specs = [pl.BlockSpec((row_count, span), lambda h: (0, h))]
    else:
        shapes = [
            jax.ShapeDtypeStruct((high - low, 8, row_count), F32),
            jax.ShapeDtypeStruct((high - low, HEAD_DIM, row_count), F32),
        ]
        out_specs = [state, accum]
    return pl.pallas_call(
        lambda *refs: attend_kernel(
            *refs, buffers=len(buffers), own=own, first=first, last=last, heads=heads
        ),
        grid=((high - low) // heads,),
        in_specs=specs,
        out_specs=out_specs,
        out_shape=shapes,
        name=name,
        compiler_params=pltpu.CompilerParams(vmem_limit_bytes=48 << 20),
        cost_estimate=pl.CostEstimate(
            flops=4 * row_count * count * width,
            bytes_accessed=8 * row_count * width,
            transcendentals=row_count * count * (high - low),
        ),
    )(*operands)


def per_device(query_vectors, key_vectors, value_vectors, band_table, out_weight):
    row_count, width = query_vectors.shape
    block_count = lax.axis_size("tm")
    group_count = lax.axis_size("head")
    my_block = lax.axis_index("tm")
    my_group = lax.axis_index("head")
    table_row = lax.dynamic_index_in_dim(band_table, my_block, 0, keepdims=False)

    def move(array, block_to, group_to=lambda h: h):
        route = []
        for t in range(block_count):
            for h in range(group_count):
                to = block_to(t)
                if to is not None and 0 <= to < block_count:
                    route.append((t * group_count + h, to * group_count + group_to(h)))
        return lax.ppermute(array, AXES, route)

    def bias_of(pieces):
        blocks = jnp.stack([jnp.asarray(block, jnp.int32) for block, _, _ in pieces])
        number = np.concatenate([np.full(n, i) for i, (_, _, n) in enumerate(pieces)])
        rank = np.concatenate([np.arange(a, a + n) for _, a, n in pieces]).astype(np.int32)
        member = jnp.asarray(number[None, :] == np.arange(len(pieces))[:, None])
        here = jnp.arange(block_count, dtype=jnp.int32)[None, :] == blocks[:, None]
        band = jnp.sum(jnp.where(here, table_row[None, :], 0), axis=1)
        kept = jnp.where(jnp.any(here, axis=1), jnp.right_shift(jnp.int32(row_count), band), 0)
        limit = jnp.sum(jnp.where(member, kept[:, None], 0), axis=0)
        bias = jnp.where(jnp.asarray(rank) < limit, 0.0, MASKED).astype(F32)
        return jnp.broadcast_to(bias[:, None], (rank.size, HEAD_DIM))

    def within(block):
        return (block >= 0) & (block < block_count)

    head_count = width // HEAD_DIM
    core = lambda h: h ^ 1
    same = lambda t: t
    mine = my_group % 2
    level = my_group // 2
    out_width = out_weight.shape[1] // group_count
    away, home = (2 * (1 - level) + mine, 2 * level + mine)
    moved = move(out_weight, same, core)
    near = row_count // 2
    own_pair = (key_vectors, value_vectors)

    def further(buffers, pieces, carry, name):
        return attend(
            query_vectors, None, buffers, bias_of(pieces), carry, False, 0, head_count, name
        )

    if block_count == 8:
        a, ab = (row_count // 8, row_count // 4)
        side = jnp.where(my_block % 2 == 0, 1, -1)
        far_way = lambda t: t + 2 if t % 2 == 0 else t - 2
        near_way = lambda t: t - 2 if t % 2 == 0 else t + 2
        partner, two, opposite = (my_block ^ 1, my_block ^ 4, my_block ^ 6)
        far_block, near_block = (my_block - 2 * side, my_block + 2 * side)
        adjacent, far_cross = (my_block - side, my_block + 3 * side)
        at_end = (my_block < 2) | (my_block >= block_count - 2)
        none = jnp.int32(-1)
        three = jnp.where(at_end, opposite, none)

        sent, sent_ab, sent_a = pack(key_vectors, value_vectors, [(0, near), (0, ab), (0, a)])
        x_rows = move(sent, lambda t: t ^ 1)
        z_far = move(sent_ab, far_way)
        z_near = move(sent_ab, near_way)
        z_two = move(sent_a, lambda t: t ^ 4)
        carry = attend(query_vectors, own_pair, [], None, None, False, 0, head_count, "own")
        x_rows, z_far, z_near, state = lax.optimization_barrier((x_rows, z_far, z_near, carry[0]))
        carry = (state, carry[1])
        near_b = move(x_rows[:, a:ab], far_way)
        near_c = move(x_rows[:, ab:], far_way)
        flags = jnp.stack([within(far_block), within(near_block)]).astype(jnp.int32)
        crossed = move(gather(flags, z_far, z_near, z_two), lambda t: t ^ 1)
        z_three = move(z_two, lambda t: {4: 6, 5: 7, 2: 0, 3: 1}.get(t))
        carry = further(
            [x_rows, z_far, z_near, z_two],
            [(partner, 0, near), (far_block, 0, ab), (near_block, 0, ab), (two, 0, a)],
            carry,
            "first",
        )
        near_b, z_three, state, out_weight, moved = lax.optimization_barrier(
            (near_b, z_three, carry[0], out_weight, moved)
        )
        carry = (state, carry[1])
        cross_last = move(jnp.where(at_end, z_three, z_two), lambda t: t ^ 1)
        chain_b = move(near_b, far_way)
        carry = further(
            [near_b, near_c, z_three],
            [(adjacent, a, ab - a), (adjacent, ab, near - ab), (three, 0, a)],
            carry,
            "middle",
        )
        buffers = [crossed, cross_last, chain_b]
        pieces = [
            (jnp.where(within(far_cross), far_cross, two ^ 1), 0, a),
            (far_cross, a, ab - a),
            (jnp.where(within(adjacent), adjacent, two ^ 1), 0, a),
            (jnp.where(at_end, opposite ^ 1, two ^ 1), 0, a),
            (my_block - 3 * side, a, ab - a),
        ]
    else:
        (packed,) = pack(key_vectors, value_vectors, [(0, near)])
        received, pieces = ([], [])
        for distance in range(1, block_count):
            rows = row_count >> distance.bit_length()
            for sign in (1, -1):
                received.append(move(packed[:, :rows], lambda t: t + sign * distance))
                pieces.append((my_block - sign * distance, 0, rows))
        carry = attend(query_vectors, own_pair, [], None, None, False, 0, head_count, "own")
        carry = further([jnp.concatenate(received[:2], axis=1)], pieces[:2], carry, "first")
        buffers, pieces = ([jnp.concatenate(received[2:], axis=1)], pieces[2:])

    def block_of(weight, number):
        return lax.dynamic_slice_in_dim(weight, number * out_width, out_width, 1)

    weights = lax.optimization_barrier(
        [block_of(weight, number) for weight in (out_weight, moved) for number in (away, home)]
    )
    bias = bias_of(pieces)
    cut = head_count // 2
    parts = []
    for low, high in ((0, cut), (cut, head_count)):
        (part,) = attend(
            query_vectors, None, buffers, bias, carry, True, low, high, f"last{low}"
        )
        parts.append((part, move(part, same, core), low * HEAD_DIM, high * HEAD_DIM))

    def project(index, first, last):
        total = 0.0
        for part, other, low, high in parts:
            total = total + jnp.dot(
                part, weights[index][low:high, first:last], preferred_element_type=F32
            )
            total = total + jnp.dot(
                other, weights[index + 2][low:high, first:last], preferred_element_type=F32
            )
        return total

    half = out_width // 2
    arrived = [
        move(project(0, first, first + half).astype(BF16), same, lambda h: h ^ 2)
        for first in (0, half)
    ]
    kept, arrived[0] = lax.optimization_barrier((project(1, 0, out_width), arrived[0]))
    return (kept + jnp.concatenate(arrived, axis=1).astype(F32)).astype(BF16)


def solution(mesh):
    in_specs = (P("tm", "head"), P("tm", "head"), P("tm", "head"), P(), P("head", None))
    out_specs = P("tm", "head")
    return jax.shard_map(
        per_device, mesh=mesh, in_specs=in_specs, out_specs=out_specs, check_vma=False
    )
```

```python
import math

import jax
import jax.numpy as jnp
import numpy as np
from jax import lax
from jax.experimental import pallas as pl
from jax.experimental.pallas import tpu as pltpu
from jax.sharding import PartitionSpec as P

HEAD_DIM = 128
MASKED = -1e30
AXES = ("tm", "head")
F32 = jnp.float32
BF16 = jnp.bfloat16


def pack_kernel(key_ref, value_ref, *out_refs, cuts):
    row_count = key_ref.shape[0]
    picks = row_count // 2
    rank = lax.broadcasted_iota(jnp.int32, (picks, 1), 0)
    place = jnp.zeros_like(rank)
    step = 1
    while step < picks:
        stride = row_count // (2 * step)
        place = jnp.where(rank >= step, (2 * (rank - step) + 1) * stride, place)
        step *= 2
    column = lax.broadcasted_iota(jnp.int32, (picks, row_count), 1)
    choose = jnp.where(place == column, 1.0, 0.0).astype(BF16)
    for plane, source in enumerate((key_ref, value_ref)):
        picked = jnp.dot(choose, source[...], preferred_element_type=F32).astype(BF16)
        for out_ref, (low, high) in zip(out_refs, cuts):
            out_ref[plane] = picked[low:high]


def pack(key_vectors, value_vectors, cuts):
    row_count, width = key_vectors.shape
    tile = width // 2
    return pl.pallas_call(
        lambda *refs: pack_kernel(*refs, cuts=cuts),
        grid=(width // tile,),
        in_specs=[pl.BlockSpec((row_count, tile), lambda j: (0, j))] * 2,
        out_specs=[
            pl.BlockSpec((2, high - low, tile), lambda j: (0, 0, j)) for low, high in cuts
        ],
        out_shape=[jax.ShapeDtypeStruct((2, high - low, width), BF16) for low, high in cuts],
        name="pack",
        compiler_params=pltpu.CompilerParams(vmem_limit_bytes=48 << 20),
        cost_estimate=pl.CostEstimate(
            flops=2 * row_count * row_count * width,
            bytes_accessed=8 * row_count * width,
            transcendentals=0,
        ),
    )(key_vectors, value_vectors)


def attend_kernel(*refs, buffers, own, first, last, low, high):
    refs = list(refs)
    query_ref = refs.pop(0)
    own_refs = [refs.pop(0), refs.pop(0)] if own else None
    packed_refs = [refs.pop(0) for _ in range(buffers)]
    bias_ref = refs.pop(0) if buffers else None
    state_in, accum_in = (None, None) if first else (refs.pop(0), refs.pop(0))
    query_count = query_ref.shape[0]
    factor = math.log2(math.e) / math.sqrt(HEAD_DIM)
    together = 2

    def one(head):
        span = pl.ds(pl.multiple_of((head + low) * HEAD_DIM, HEAD_DIM), HEAD_DIM)
        if own:
            key, value = (own_refs[0][:, span], own_refs[1][:, span])
        else:
            key = jnp.concatenate([ref[0, :, span] for ref in packed_refs], axis=0)
            value = jnp.concatenate([ref[1, :, span] for ref in packed_refs], axis=0)
        scores = lax.dot_general(
            key, query_ref[:, span], (((1,), (1,)), ((), ())), preferred_element_type=F32
        )
        if buffers:
            scores = scores + jnp.concatenate([bias_ref[...]] * (query_count // HEAD_DIM), axis=1)
        top = jnp.max(scores, axis=0, keepdims=True)
        if not first:
            state = state_in[head + low]
            top = jnp.maximum(top, state[0:1])
            shrink = jnp.exp2((state[0:1] - top) * factor)
        weights = jnp.exp2(scores * factor - top * factor)
        total = jnp.sum(weights, axis=0, keepdims=True)
        accum = jnp.dot(value.T, weights.astype(BF16), preferred_element_type=F32)
        if not first:
            total = total + shrink * state[1:2]
            accum = accum + shrink * accum_in[head + low]
        if last:
            out = pl.ds(pl.multiple_of(head * HEAD_DIM, HEAD_DIM), HEAD_DIM)
            refs[0][:, out] = (accum / total).T.astype(BF16)
        else:
            refs[0][head, 0:1, :] = top
            refs[0][head, 1:2, :] = total
            refs[1][head] = accum

    def several(step, nothing):
        for member in range(together):
            one(step * together + member)
        return nothing

    lax.fori_loop(0, (high - low) // together, several, 0)


def attend(query_vectors, own_pair, buffers, bias, carry, last, low, high, name):
    row_count = query_vectors.shape[0]
    own = own_pair is not None
    first = carry is None
    operands = [query_vectors] + (list(own_pair) if own else list(buffers) + [bias])
    operands += [] if first else list(carry)
    count = row_count if own else bias.shape[0]
    width = (high - low) * HEAD_DIM
    if last:
        shapes = [jax.ShapeDtypeStruct((row_count, width), BF16)]
    else:
        shapes = [
            jax.ShapeDtypeStruct((high - low, 8, row_count), F32),
            jax.ShapeDtypeStruct((high - low, HEAD_DIM, row_count), F32),
        ]
    held = pl.BlockSpec(memory_space=pltpu.VMEM)
    return pl.pallas_call(
        lambda *refs: attend_kernel(
            *refs, buffers=len(buffers), own=own, first=first, last=last, low=low, high=high
        ),
        in_specs=[held] * len(operands),
        out_specs=[held] * len(shapes),
        out_shape=shapes,
        name=name,
        compiler_params=pltpu.CompilerParams(vmem_limit_bytes=16 << 20),
        cost_estimate=pl.CostEstimate(
            flops=4 * row_count * count * width,
            bytes_accessed=8 * row_count * width,
            transcendentals=row_count * count * (high - low),
        ),
    )(*operands)


def per_device(query_vectors, key_vectors, value_vectors, band_table, out_weight):
    row_count, width = query_vectors.shape
    block_count = lax.axis_size("tm")
    group_count = lax.axis_size("head")
    my_block = lax.axis_index("tm")
    my_group = lax.axis_index("head")
    table_row = lax.dynamic_index_in_dim(band_table, my_block, 0, keepdims=False)

    def move(array, block_to, group_to=lambda h: h):
        route = []
        for t in range(block_count):
            for h in range(group_count):
                to = block_to(t)
                if to is not None and 0 <= to < block_count:
                    route.append((t * group_count + h, to * group_count + group_to(h)))
        return lax.ppermute(array, AXES, route)

    def bias_of(pieces):
        blocks = jnp.stack([jnp.asarray(block, jnp.int32) for block, _, _ in pieces])
        number = np.concatenate([np.full(n, i) for i, (_, _, n) in enumerate(pieces)])
        rank = np.concatenate([np.arange(a, a + n) for _, a, n in pieces]).astype(np.int32)
        member = jnp.asarray(number[None, :] == np.arange(len(pieces))[:, None])
        here = jnp.arange(block_count, dtype=jnp.int32)[None, :] == blocks[:, None]
        band = jnp.sum(jnp.where(here, table_row[None, :], 0), axis=1)
        kept = jnp.where(jnp.any(here, axis=1), jnp.right_shift(jnp.int32(row_count), band), 0)
        limit = jnp.sum(jnp.where(member, kept[:, None], 0), axis=0)
        bias = jnp.where(jnp.asarray(rank) < limit, 0.0, MASKED).astype(F32)
        return jnp.broadcast_to(bias[:, None], (rank.size, HEAD_DIM))

    def within(block):
        return (block >= 0) & (block < block_count)

    head_count = width // HEAD_DIM
    core = lambda h: h ^ 1
    same = lambda t: t
    mine = my_group % 2
    level = my_group // 2
    out_width = out_weight.shape[1] // group_count
    away, home = (2 * (1 - level) + mine, 2 * level + mine)
    moved = move(out_weight, same, core)
    near = row_count // 2
    own_pair = (key_vectors, value_vectors)

    def further(buffers, pieces, carry, name):
        return attend(
            query_vectors, None, buffers, bias_of(pieces), carry, False, 0, head_count, name
        )

    def blocks_of(*sources):
        return [
            lax.dynamic_slice_in_dim(source, number * out_width, out_width, 1)
            for source in sources
            for number in (away, home)
        ]

    if block_count == 8:
        a, ab = (row_count // 8, row_count // 4)
        side = jnp.where(my_block % 2 == 0, 1, -1)
        far_of = lambda t: t - 2 if t % 2 == 0 else t + 2
        near_of = lambda t: t + 2 if t % 2 == 0 else t - 2
        twin_if = lambda source: lambda t: t ^ 1 if 0 <= source(t) < block_count else None
        ends = (0, 1, block_count - 2, block_count - 1)
        partner, two, opposite = (my_block ^ 1, my_block ^ 4, my_block ^ 6)
        far_block, near_block = (my_block - 2 * side, my_block + 2 * side)
        adjacent, far_cross = (my_block - side, my_block + 3 * side)
        at_end = (my_block < 2) | (my_block >= block_count - 2)
        three = jnp.where(at_end, opposite, -1)

        sent, sent_ab, sent_a = pack(key_vectors, value_vectors, [(0, near), (0, ab), (0, a)])
        x_rows = move(sent, lambda t: t ^ 1)
        z_far = move(sent_ab, near_of)
        z_near = move(sent_ab, far_of)
        z_two = move(sent_a, lambda t: t ^ 4)
        carry = attend(query_vectors, own_pair, [], None, None, False, 0, head_count, "own")
        z_far, z_near, state, out_weight, moved = lax.optimization_barrier(
            (z_far, z_near, carry[0], out_weight, moved)
        )
        cross_far = move(z_far, twin_if(far_of))
        cross_near = move(z_near[:, :a], twin_if(near_of))
        weights = blocks_of(out_weight, moved)
        x_rows, z_two, state, weights = lax.optimization_barrier((x_rows, z_two, state, weights))
        near_bc = move(x_rows[:, a:], near_of)
        cross_two = move(z_two, lambda t: t ^ 1)
        z_three = move(z_two, lambda t: {4: 6, 5: 7, 2: 0, 3: 1}.get(t))
        carry = further(
            [x_rows, z_far, z_near, z_two],
            [(partner, 0, near), (far_block, 0, ab), (near_block, 0, ab), (two, 0, a)],
            (state, carry[1]),
            "first",
        )
        z_three, state = lax.optimization_barrier((z_three, carry[0]))
        cross_three = move(z_three, lambda t: t ^ 1 if t in ends else None)
        near_bc, state = lax.optimization_barrier((near_bc, state))
        chain_b = move(near_bc[:, : ab - a], near_of)
        carry = further(
            [near_bc, z_three],
            [(adjacent, a, near - a), (three, 0, a)],
            (state, carry[1]),
            "middle",
        )
        buffers = [cross_far, cross_near, cross_two, cross_three, chain_b]
        pieces = [
            (far_cross, 0, ab),
            (adjacent, 0, a),
            (two ^ 1, 0, a),
            (jnp.where(at_end, opposite ^ 1, -1), 0, a),
            (my_block - 3 * side, a, ab - a),
        ]
    else:
        (packed,) = pack(key_vectors, value_vectors, [(0, near)])
        received, pieces = ([], [])
        for distance in range(1, block_count):
            rows = row_count >> distance.bit_length()
            for sign in (1, -1):
                received.append(move(packed[:, :rows], lambda t: t + sign * distance))
                pieces.append((my_block - sign * distance, 0, rows))
        carry = attend(query_vectors, own_pair, [], None, None, False, 0, head_count, "own")
        carry = further([jnp.concatenate(received[:2], axis=1)], pieces[:2], carry, "first")
        buffers, pieces = ([jnp.concatenate(received[2:], axis=1)], pieces[2:])
        weights = lax.optimization_barrier(blocks_of(out_weight, moved))

    bias = bias_of(pieces)
    cut = 2 * ((head_count + 2) // 4)
    parts = []
    for low, high in ((0, cut), (cut, head_count)):
        (part,) = attend(
            query_vectors, None, buffers, bias, carry, True, low, high, f"last{low}"
        )
        parts.append((part, move(part, same, core), low * HEAD_DIM, high * HEAD_DIM))

    def project(index, first, last):
        total = 0.0
        for part, other, low, high in parts:
            total = total + jnp.dot(
                part, weights[index][low:high, first:last], preferred_element_type=F32
            )
            total = total + jnp.dot(
                other, weights[index + 2][low:high, first:last], preferred_element_type=F32
            )
        return total

    half = out_width // 2
    sent = [project(0, first, first + half).astype(BF16) for first in (0, half)]
    sent[1], held = lax.optimization_barrier((sent[1], [part[:2] for part in parts]))
    parts = [kept + part[2:] for kept, part in zip(held, parts)]
    arrived = [move(block, same, lambda h: h ^ 2) for block in sent]
    kept, arrived[0] = lax.optimization_barrier((project(1, 0, out_width), arrived[0]))
    return (kept + jnp.concatenate(arrived, axis=1).astype(F32)).astype(BF16)


def solution(mesh):
    in_specs = (P("tm", "head"), P("tm", "head"), P("tm", "head"), P(), P("head", None))
    out_specs = P("tm", "head")
    return jax.shard_map(
        per_device, mesh=mesh, in_specs=in_specs, out_specs=out_specs, check_vma=False
    )
```

```python
import math

import jax
import jax.numpy as jnp
import numpy as np
from jax import lax
from jax.experimental import pallas as pl
from jax.experimental.pallas import tpu as pltpu
from jax.sharding import PartitionSpec as P

HEAD_DIM = 128
MASKED = -1e30
AXES = ("tm", "head")
F32 = jnp.float32
BF16 = jnp.bfloat16


def pack_kernel(key_ref, value_ref, *out_refs, cuts):
    row_count = key_ref.shape[0]
    picks = row_count // 2
    rank = lax.broadcasted_iota(jnp.int32, (picks, 1), 0)
    place = jnp.zeros_like(rank)
    step = 1
    while step < picks:
        stride = row_count // (2 * step)
        place = jnp.where(rank >= step, (2 * (rank - step) + 1) * stride, place)
        step *= 2
    column = lax.broadcasted_iota(jnp.int32, (picks, row_count), 1)
    choose = jnp.where(place == column, 1.0, 0.0).astype(BF16)
    for plane, source in enumerate((key_ref, value_ref)):
        picked = jnp.dot(choose, source[...], preferred_element_type=F32).astype(BF16)
        for out_ref, (low, high) in zip(out_refs, cuts):
            out_ref[plane] = picked[low:high]


def pack(key_vectors, value_vectors, cuts):
    row_count, width = key_vectors.shape
    tile = width // 2
    return pl.pallas_call(
        lambda *refs: pack_kernel(*refs, cuts=cuts),
        grid=(width // tile,),
        in_specs=[pl.BlockSpec((row_count, tile), lambda j: (0, j))] * 2,
        out_specs=[
            pl.BlockSpec((2, high - low, tile), lambda j: (0, 0, j)) for low, high in cuts
        ],
        out_shape=[jax.ShapeDtypeStruct((2, high - low, width), BF16) for low, high in cuts],
        name="pack",
        compiler_params=pltpu.CompilerParams(vmem_limit_bytes=48 << 20),
        cost_estimate=pl.CostEstimate(
            flops=2 * row_count * row_count * width,
            bytes_accessed=8 * row_count * width,
            transcendentals=0,
        ),
    )(key_vectors, value_vectors)


def gather_kernel(flag_ref, far_ref, near_ref, two_ref, out_ref):
    a = two_ref.shape[1]
    ab = far_ref.shape[1]
    far_here, near_here = (flag_ref[0] != 0, flag_ref[1] != 0)
    for plane in range(2):
        two = two_ref[plane]
        out_ref[plane, :a] = jnp.where(far_here, far_ref[plane, :a], two)
        out_ref[plane, a:ab] = far_ref[plane, a:]
        out_ref[plane, ab:] = jnp.where(near_here, near_ref[plane, :a], two)


def gather(flags, far, near, two):
    rows = far.shape[1] + two.shape[1]
    width = two.shape[2]
    held = pl.BlockSpec(memory_space=pltpu.VMEM)
    return pl.pallas_call(
        gather_kernel,
        in_specs=[pl.BlockSpec(memory_space=pltpu.SMEM), held, held, held],
        out_specs=held,
        out_shape=jax.ShapeDtypeStruct((2, rows, width), BF16),
        name="gather",
        cost_estimate=pl.CostEstimate(flops=0, bytes_accessed=8 * rows * width, transcendentals=0),
    )(flags, far, near, two)


def attend_kernel(*refs, buffers, own, first, last, low, high):
    refs = list(refs)
    query_ref = refs.pop(0)
    own_refs = [refs.pop(0), refs.pop(0)] if own else None
    packed_refs = [refs.pop(0) for _ in range(buffers)]
    bias_ref = refs.pop(0) if buffers else None
    state_in, accum_in = (None, None) if first else (refs.pop(0), refs.pop(0))
    query_count = query_ref.shape[0]
    factor = math.log2(math.e) / math.sqrt(HEAD_DIM)
    together = 2

    def one(head):
        span = pl.ds(pl.multiple_of((head + low) * HEAD_DIM, HEAD_DIM), HEAD_DIM)
        if own:
            key, value = (own_refs[0][:, span], own_refs[1][:, span])
        else:
            key = jnp.concatenate([ref[0, :, span] for ref in packed_refs], axis=0)
            value = jnp.concatenate([ref[1, :, span] for ref in packed_refs], axis=0)
        scores = lax.dot_general(
            key, query_ref[:, span], (((1,), (1,)), ((), ())), preferred_element_type=F32
        )
        if buffers:
            scores = scores + jnp.concatenate([bias_ref[...]] * (query_count // HEAD_DIM), axis=1)
        top = jnp.max(scores, axis=0, keepdims=True)
        if not first:
            state = state_in[head + low]
            top = jnp.maximum(top, state[0:1])
            shrink = jnp.exp2((state[0:1] - top) * factor)
        weights = jnp.exp2(scores * factor - top * factor)
        total = jnp.sum(weights, axis=0, keepdims=True)
        accum = jnp.dot(value.T, weights.astype(BF16), preferred_element_type=F32)
        if not first:
            total = total + shrink * state[1:2]
            accum = accum + shrink * accum_in[head + low]
        if last:
            out = pl.ds(pl.multiple_of(head * HEAD_DIM, HEAD_DIM), HEAD_DIM)
            refs[0][:, out] = (accum / total).T.astype(BF16)
        else:
            refs[0][head, 0:1, :] = top
            refs[0][head, 1:2, :] = total
            refs[1][head] = accum

    def several(step, nothing):
        for member in range(together):
            one(step * together + member)
        return nothing

    lax.fori_loop(0, (high - low) // together, several, 0)


def attend(query_vectors, own_pair, buffers, bias, carry, last, low, high, name):
    row_count = query_vectors.shape[0]
    own = own_pair is not None
    first = carry is None
    operands = [query_vectors] + (list(own_pair) if own else list(buffers) + [bias])
    operands += [] if first else list(carry)
    count = row_count if own else bias.shape[0]
    width = (high - low) * HEAD_DIM
    if last:
        shapes = [jax.ShapeDtypeStruct((row_count, width), BF16)]
    else:
        shapes = [
            jax.ShapeDtypeStruct((high - low, 8, row_count), F32),
            jax.ShapeDtypeStruct((high - low, HEAD_DIM, row_count), F32),
        ]
    held = pl.BlockSpec(memory_space=pltpu.VMEM)
    return pl.pallas_call(
        lambda *refs: attend_kernel(
            *refs, buffers=len(buffers), own=own, first=first, last=last, low=low, high=high
        ),
        in_specs=[held] * len(operands),
        out_specs=[held] * len(shapes),
        out_shape=shapes,
        name=name,
        compiler_params=pltpu.CompilerParams(vmem_limit_bytes=16 << 20),
        cost_estimate=pl.CostEstimate(
            flops=4 * row_count * count * width,
            bytes_accessed=8 * row_count * width,
            transcendentals=row_count * count * (high - low),
        ),
    )(*operands)


def per_device(query_vectors, key_vectors, value_vectors, band_table, out_weight):
    row_count, width = query_vectors.shape
    block_count = lax.axis_size("tm")
    group_count = lax.axis_size("head")
    my_block = lax.axis_index("tm")
    my_group = lax.axis_index("head")
    table_row = lax.dynamic_index_in_dim(band_table, my_block, 0, keepdims=False)

    def move(array, block_to, group_to=lambda h: h):
        route = []
        for t in range(block_count):
            for h in range(group_count):
                to = block_to(t)
                if to is not None and 0 <= to < block_count:
                    route.append((t * group_count + h, to * group_count + group_to(h)))
        return lax.ppermute(array, AXES, route)

    def bias_of(pieces):
        blocks = jnp.stack([jnp.asarray(block, jnp.int32) for block, _, _ in pieces])
        number = np.concatenate([np.full(n, i) for i, (_, _, n) in enumerate(pieces)])
        rank = np.concatenate([np.arange(a, a + n) for _, a, n in pieces]).astype(np.int32)
        member = jnp.asarray(number[None, :] == np.arange(len(pieces))[:, None])
        here = jnp.arange(block_count, dtype=jnp.int32)[None, :] == blocks[:, None]
        band = jnp.sum(jnp.where(here, table_row[None, :], 0), axis=1)
        kept = jnp.where(jnp.any(here, axis=1), jnp.right_shift(jnp.int32(row_count), band), 0)
        limit = jnp.sum(jnp.where(member, kept[:, None], 0), axis=0)
        bias = jnp.where(jnp.asarray(rank) < limit, 0.0, MASKED).astype(F32)
        return jnp.broadcast_to(bias[:, None], (rank.size, HEAD_DIM))

    def within(block):
        return (block >= 0) & (block < block_count)

    head_count = width // HEAD_DIM
    core = lambda h: h ^ 1
    same = lambda t: t
    mine = my_group % 2
    level = my_group // 2
    out_width = out_weight.shape[1] // group_count
    away, home = (2 * (1 - level) + mine, 2 * level + mine)
    near = row_count // 2
    own_pair = (key_vectors, value_vectors)

    def further(buffers, pieces, carry, name):
        return attend(
            query_vectors, None, buffers, bias_of(pieces), carry, False, 0, head_count, name
        )

    def blocks_of(*sources):
        return [
            lax.dynamic_slice_in_dim(source, number * out_width, out_width, 1)
            for source in sources
            for number in (away, home)
        ]

    if block_count == 8:
        a, ab = (row_count // 8, row_count // 4)
        side = jnp.where(my_block % 2 == 0, 1, -1)
        far_of = lambda t: t - 2 if t % 2 == 0 else t + 2
        near_of = lambda t: t + 2 if t % 2 == 0 else t - 2
        ends = (0, 1, block_count - 2, block_count - 1)
        partner, two, opposite = (my_block ^ 1, my_block ^ 4, my_block ^ 6)
        far_block, near_block = (my_block - 2 * side, my_block + 2 * side)
        adjacent, far_cross = (my_block - side, my_block + 3 * side)
        at_end = (my_block < 2) | (my_block >= block_count - 2)
        three = jnp.where(at_end, opposite, -1)

        sent, sent_ab, sent_a = pack(key_vectors, value_vectors, [(0, near), (0, ab), (0, a)])
        x_rows = move(sent, lambda t: t ^ 1)
        z_far = move(sent_ab, near_of)
        z_near = move(sent_ab, far_of)
        z_two = move(sent_a, lambda t: t ^ 4)
        z_three = move(sent_a, lambda t: t ^ 6 if t in ends else None)
        carry = attend(query_vectors, own_pair, [], None, None, False, 0, head_count, "own")
        x_rows, z_far, z_near, z_two, state, out_weight = lax.optimization_barrier(
            (x_rows, z_far, z_near, z_two, carry[0], out_weight)
        )
        near_b = move(x_rows[:, a:ab], near_of)
        near_c = move(x_rows[:, ab:], near_of)
        flags = jnp.stack([within(far_block), within(near_block)]).astype(jnp.int32)
        crossed = move(gather(flags, z_far, z_near, z_two), lambda t: t ^ 1)
        cross_last = move(jnp.where(at_end, z_three, z_two), lambda t: t ^ 1)
        moved = move(out_weight, same, core)
        carry = further(
            [x_rows, z_far, z_near, z_two, z_three],
            [
                (partner, 0, near),
                (far_block, 0, ab),
                (near_block, 0, ab),
                (two, 0, a),
                (three, 0, a),
            ],
            (state, carry[1]),
            "first",
        )
        near_b, state, moved = lax.optimization_barrier((near_b, carry[0], moved))
        chain_b = move(near_b, near_of)
        weights = lax.optimization_barrier(blocks_of(out_weight, moved))
        carry = further(
            [near_b, near_c],
            [(adjacent, a, ab - a), (adjacent, ab, near - ab)],
            (state, carry[1]),
            "middle",
        )
        buffers = [crossed, cross_last, chain_b]
        pieces = [
            (jnp.where(within(far_cross), far_cross, two ^ 1), 0, a),
            (far_cross, a, ab - a),
            (jnp.where(within(adjacent), adjacent, two ^ 1), 0, a),
            (jnp.where(at_end, opposite ^ 1, two ^ 1), 0, a),
            (my_block - 3 * side, a, ab - a),
        ]
    else:
        (packed,) = pack(key_vectors, value_vectors, [(0, near)])
        received, pieces = ([], [])
        for distance in range(1, block_count):
            rows = row_count >> distance.bit_length()
            for sign in (1, -1):
                received.append(move(packed[:, :rows], lambda t: t + sign * distance))
                pieces.append((my_block - sign * distance, 0, rows))
        carry = attend(query_vectors, own_pair, [], None, None, False, 0, head_count, "own")
        carry = further([jnp.concatenate(received[:2], axis=1)], pieces[:2], carry, "first")
        buffers, pieces = ([jnp.concatenate(received[2:], axis=1)], pieces[2:])
        moved = move(out_weight, same, core)
        weights = lax.optimization_barrier(blocks_of(out_weight, moved))

    bias = bias_of(pieces)
    cut = 2 * ((head_count + 2) // 4)
    parts = []
    for low, high in ((0, cut), (cut, head_count)):
        (part,) = attend(
            query_vectors, None, buffers, bias, carry, True, low, high, f"last{low}"
        )
        parts.append((part, move(part, same, core), low * HEAD_DIM, high * HEAD_DIM))

    def project(index, first, last):
        total = 0.0
        for part, other, low, high in parts:
            total = total + jnp.dot(
                part, weights[index][low:high, first:last], preferred_element_type=F32
            )
            total = total + jnp.dot(
                other, weights[index + 2][low:high, first:last], preferred_element_type=F32
            )
        return total

    half = out_width // 2
    sent = [project(0, first, first + half).astype(BF16) for first in (0, half)]
    sent[1], held = lax.optimization_barrier((sent[1], [part[:2] for part in parts]))
    parts = [kept + part[2:] for kept, part in zip(held, parts)]
    arrived = [move(block, same, lambda h: h ^ 2) for block in sent]
    kept, arrived[0] = lax.optimization_barrier((project(1, 0, out_width), arrived[0]))
    return (kept + jnp.concatenate(arrived, axis=1).astype(F32)).astype(BF16)


def solution(mesh):
    in_specs = (P("tm", "head"), P("tm", "head"), P("tm", "head"), P(), P("head", None))
    out_specs = P("tm", "head")
    return jax.shard_map(
        per_device, mesh=mesh, in_specs=in_specs, out_specs=out_specs, check_vma=False
    )
```

```python
import math

import jax
import jax.numpy as jnp
import numpy as np
from jax import lax
from jax.experimental import pallas as pl
from jax.experimental.pallas import tpu as pltpu
from jax.sharding import PartitionSpec as P

HEAD_DIM = 128
MASKED = -1e30
AXES = ("tm", "head")
F32 = jnp.float32
BF16 = jnp.bfloat16


def pack_kernel(key_ref, value_ref, *out_refs, cuts):
    row_count = key_ref.shape[0]
    picks = row_count // 2
    rank = lax.broadcasted_iota(jnp.int32, (picks, 1), 0)
    place = jnp.zeros_like(rank)
    step = 1
    while step < picks:
        stride = row_count // (2 * step)
        place = jnp.where(rank >= step, (2 * (rank - step) + 1) * stride, place)
        step *= 2
    column = lax.broadcasted_iota(jnp.int32, (picks, row_count), 1)
    choose = jnp.where(place == column, 1.0, 0.0).astype(BF16)
    for plane, source in enumerate((key_ref, value_ref)):
        picked = jnp.dot(choose, source[...], preferred_element_type=F32).astype(BF16)
        for out_ref, (low, high) in zip(out_refs, cuts):
            out_ref[plane] = picked[low:high]


def pack(key_vectors, value_vectors, cuts):
    row_count, width = key_vectors.shape
    tile = width // 2
    return pl.pallas_call(
        lambda *refs: pack_kernel(*refs, cuts=cuts),
        grid=(width // tile,),
        in_specs=[pl.BlockSpec((row_count, tile), lambda j: (0, j))] * 2,
        out_specs=[
            pl.BlockSpec((2, high - low, tile), lambda j: (0, 0, j)) for low, high in cuts
        ],
        out_shape=[jax.ShapeDtypeStruct((2, high - low, width), BF16) for low, high in cuts],
        name="pack",
        compiler_params=pltpu.CompilerParams(vmem_limit_bytes=48 << 20),
        cost_estimate=pl.CostEstimate(
            flops=2 * row_count * row_count * width,
            bytes_accessed=8 * row_count * width,
            transcendentals=0,
        ),
    )(key_vectors, value_vectors)


def attend_kernel(*refs, buffers, own, first, last, low, high):
    refs = list(refs)
    query_ref = refs.pop(0)
    own_refs = [refs.pop(0), refs.pop(0)] if own else None
    packed_refs = [refs.pop(0) for _ in range(buffers)]
    bias_ref = refs.pop(0) if buffers else None
    state_in, accum_in = (None, None) if first else (refs.pop(0), refs.pop(0))
    query_count = query_ref.shape[0]
    factor = math.log2(math.e) / math.sqrt(HEAD_DIM)
    together = 2

    def one(head):
        span = pl.ds(pl.multiple_of((head + low) * HEAD_DIM, HEAD_DIM), HEAD_DIM)
        if own:
            key, value = (own_refs[0][:, span], own_refs[1][:, span])
        else:
            key = jnp.concatenate([ref[0, :, span] for ref in packed_refs], axis=0)
            value = jnp.concatenate([ref[1, :, span] for ref in packed_refs], axis=0)
        scores = lax.dot_general(
            key, query_ref[:, span], (((1,), (1,)), ((), ())), preferred_element_type=F32
        )
        if buffers:
            scores = scores + jnp.concatenate([bias_ref[...]] * (query_count // HEAD_DIM), axis=1)
        top = jnp.max(scores, axis=0, keepdims=True)
        if not first:
            state = state_in[head + low]
            top = jnp.maximum(top, state[0:1])
            shrink = jnp.exp2((state[0:1] - top) * factor)
        weights = jnp.exp2(scores * factor - top * factor)
        total = jnp.sum(weights, axis=0, keepdims=True)
        accum = jnp.dot(value.T, weights.astype(BF16), preferred_element_type=F32)
        if not first:
            total = total + shrink * state[1:2]
            accum = accum + shrink * accum_in[head + low]
        if last:
            out = pl.ds(pl.multiple_of(head * HEAD_DIM, HEAD_DIM), HEAD_DIM)
            refs[0][:, out] = (accum / total).T.astype(BF16)
        else:
            refs[0][head, 0:1, :] = top
            refs[0][head, 1:2, :] = total
            refs[1][head] = accum

    def several(step, nothing):
        for member in range(together):
            one(step * together + member)
        return nothing

    lax.fori_loop(0, (high - low) // together, several, 0)


def attend(query_vectors, own_pair, buffers, bias, carry, last, low, high, name):
    row_count = query_vectors.shape[0]
    own = own_pair is not None
    first = carry is None
    operands = [query_vectors] + (list(own_pair) if own else list(buffers) + [bias])
    operands += [] if first else list(carry)
    count = row_count if own else bias.shape[0]
    width = (high - low) * HEAD_DIM
    if last:
        shapes = [jax.ShapeDtypeStruct((row_count, width), BF16)]
    else:
        shapes = [
            jax.ShapeDtypeStruct((high - low, 8, row_count), F32),
            jax.ShapeDtypeStruct((high - low, HEAD_DIM, row_count), F32),
        ]
    held = pl.BlockSpec(memory_space=pltpu.VMEM)
    return pl.pallas_call(
        lambda *refs: attend_kernel(
            *refs, buffers=len(buffers), own=own, first=first, last=last, low=low, high=high
        ),
        in_specs=[held] * len(operands),
        out_specs=[held] * len(shapes),
        out_shape=shapes,
        name=name,
        compiler_params=pltpu.CompilerParams(vmem_limit_bytes=16 << 20),
        cost_estimate=pl.CostEstimate(
            flops=0 if own else 4 * row_count * count * width,
            bytes_accessed=0 if own else 8 * row_count * width,
            transcendentals=0 if own else row_count * count * (high - low),
        ),
    )(*operands)


def per_device(query_vectors, key_vectors, value_vectors, band_table, out_weight):
    row_count, width = query_vectors.shape
    block_count = lax.axis_size("tm")
    group_count = lax.axis_size("head")
    my_block = lax.axis_index("tm")
    my_group = lax.axis_index("head")
    table_row = lax.dynamic_index_in_dim(band_table, my_block, 0, keepdims=False)

    def move(array, block_to, group_to=lambda h: h):
        route = []
        for t in range(block_count):
            for h in range(group_count):
                to = block_to(t)
                if to is not None and 0 <= to < block_count:
                    route.append((t * group_count + h, to * group_count + group_to(h)))
        return lax.ppermute(array, AXES, route)

    def bias_of(pieces):
        blocks = jnp.stack([jnp.asarray(block, jnp.int32) for block, _, _ in pieces])
        number = np.concatenate([np.full(n, i) for i, (_, _, n) in enumerate(pieces)])
        rank = np.concatenate([np.arange(a, a + n) for _, a, n in pieces]).astype(np.int32)
        member = jnp.asarray(number[None, :] == np.arange(len(pieces))[:, None])
        here = jnp.arange(block_count, dtype=jnp.int32)[None, :] == blocks[:, None]
        band = jnp.sum(jnp.where(here, table_row[None, :], 0), axis=1)
        kept = jnp.where(jnp.any(here, axis=1), jnp.right_shift(jnp.int32(row_count), band), 0)
        limit = jnp.sum(jnp.where(member, kept[:, None], 0), axis=0)
        bias = jnp.where(jnp.asarray(rank) < limit, 0.0, MASKED).astype(F32)
        return jnp.broadcast_to(bias[:, None], (rank.size, HEAD_DIM))

    def within(block):
        return (block >= 0) & (block < block_count)

    head_count = width // HEAD_DIM
    core = lambda h: h ^ 1
    same = lambda t: t
    mine = my_group % 2
    level = my_group // 2
    out_width = out_weight.shape[1] // group_count
    away, home = (2 * (1 - level) + mine, 2 * level + mine)
    moved = move(out_weight, same, core)
    near = row_count // 2
    own_pair = (key_vectors, value_vectors)

    def further(buffers, pieces, carry, name):
        return attend(
            query_vectors, None, buffers, bias_of(pieces), carry, False, 0, head_count, name
        )

    def blocks_of(*sources):
        return [
            lax.dynamic_slice_in_dim(source, number * out_width, out_width, 1)
            for source in sources
            for number in (away, home)
        ]

    if block_count == 8:
        a, ab = (row_count // 8, row_count // 4)
        side = jnp.where(my_block % 2 == 0, 1, -1)
        far_of = lambda t: t - 2 if t % 2 == 0 else t + 2
        near_of = lambda t: t + 2 if t % 2 == 0 else t - 2
        twin_if = lambda source: lambda t: t ^ 1 if 0 <= source(t) < block_count else None
        ends = (0, 1, block_count - 2, block_count - 1)
        partner, two, opposite = (my_block ^ 1, my_block ^ 4, my_block ^ 6)
        far_block, near_block = (my_block - 2 * side, my_block + 2 * side)
        adjacent, far_cross = (my_block - side, my_block + 3 * side)
        at_end = (my_block < 2) | (my_block >= block_count - 2)
        three = jnp.where(at_end, opposite, -1)

        sent, sent_ab, sent_ba, sent_a = pack(
            key_vectors, value_vectors, [(0, near), (0, ab), (0, ab), (0, a)]
        )
        x_rows = move(sent, lambda t: t ^ 1)
        z_far = move(sent_ab, near_of)
        z_near = move(sent_ba, far_of)
        z_two = move(sent_a, lambda t: t ^ 4)
        carry = attend(query_vectors, own_pair, [], None, None, False, 0, head_count, "own")
        x_rows, z_far, z_near, z_two, state, moved = lax.optimization_barrier(
            (x_rows, z_far, z_near, z_two, carry[0], moved)
        )
        cross_far = move(z_far, twin_if(far_of))
        cross_near = move(z_near[:, :a], twin_if(near_of))
        near_bc = move(x_rows[:, a:], near_of)
        cross_two = move(z_two, lambda t: t ^ 1)
        z_three = move(z_two, lambda t: {4: 6, 5: 7, 2: 0, 3: 1}.get(t))
        carry = further(
            [x_rows, z_far, z_near, z_two],
            [(partner, 0, near), (far_block, 0, ab), (near_block, 0, ab), (two, 0, a)],
            (state, carry[1]),
            "first",
        )
        z_three, state = lax.optimization_barrier((z_three, carry[0]))
        cross_three = move(z_three, lambda t: t ^ 1 if t in ends else None)
        state, out_weight, moved = lax.optimization_barrier((state, out_weight, moved))
        weights = blocks_of(out_weight, moved)
        near_bc, state, weights = lax.optimization_barrier((near_bc, state, weights))
        chain_b = move(near_bc[:, : ab - a], near_of)
        carry = further(
            [near_bc, z_three],
            [(adjacent, a, near - a), (three, 0, a)],
            (state, carry[1]),
            "middle",
        )
        buffers = [cross_far, cross_near, cross_two, cross_three, chain_b]
        pieces = [
            (far_cross, 0, ab),
            (adjacent, 0, a),
            (two ^ 1, 0, a),
            (jnp.where(at_end, opposite ^ 1, -1), 0, a),
            (my_block - 3 * side, a, ab - a),
        ]
    else:
        (packed,) = pack(key_vectors, value_vectors, [(0, near)])
        received, pieces = ([], [])
        for distance in range(1, block_count):
            rows = row_count >> distance.bit_length()
            for sign in (1, -1):
                received.append(move(packed[:, :rows], lambda t: t + sign * distance))
                pieces.append((my_block - sign * distance, 0, rows))
        carry = attend(query_vectors, own_pair, [], None, None, False, 0, head_count, "own")
        carry = further([jnp.concatenate(received[:2], axis=1)], pieces[:2], carry, "first")
        buffers, pieces = ([jnp.concatenate(received[2:], axis=1)], pieces[2:])
        weights = lax.optimization_barrier(blocks_of(out_weight, moved))

    bias = bias_of(pieces)
    cut = 2 * ((head_count + 2) // 4)
    parts = []
    for low, high in ((0, cut), (cut, head_count)):
        (part,) = attend(
            query_vectors, None, buffers, bias, carry, True, low, high, f"last{low}"
        )
        bias, part = lax.optimization_barrier((bias, part))
        parts.append((part, move(part, same, core), low * HEAD_DIM, high * HEAD_DIM))

    def project(index, first, last):
        total = 0.0
        for part, other, low, high in parts:
            total = total + jnp.dot(
                part, weights[index][low:high, first:last], preferred_element_type=F32
            )
            total = total + jnp.dot(
                other, weights[index + 2][low:high, first:last], preferred_element_type=F32
            )
        return total

    half = out_width // 2
    sent = [project(0, first, first + half).astype(BF16) for first in (0, half)]
    sent[1], held = lax.optimization_barrier((sent[1], [part[:2] for part in parts]))
    parts = [kept + part[2:] for kept, part in zip(held, parts)]
    arrived = [move(block, same, lambda h: h ^ 2) for block in sent]
    kept, arrived[0] = lax.optimization_barrier((project(1, 0, out_width), arrived[0]))
    return (kept + jnp.concatenate(arrived, axis=1).astype(F32)).astype(BF16)


def solution(mesh):
    in_specs = (P("tm", "head"), P("tm", "head"), P("tm", "head"), P(), P("head", None))
    out_specs = P("tm", "head")
    return jax.shard_map(
        per_device, mesh=mesh, in_specs=in_specs, out_specs=out_specs, check_vma=False
    )
```

```python
import math

import jax
import jax.numpy as jnp
import numpy as np
from jax import lax
from jax.experimental import pallas as pl
from jax.experimental.pallas import tpu as pltpu
from jax.sharding import PartitionSpec as P

HEAD_DIM = 128
MASKED = -1e30
AXES = ("tm", "head")
F32 = jnp.float32
BF16 = jnp.bfloat16


def pack_kernel(key_ref, value_ref, *out_refs, cuts):
    row_count = key_ref.shape[0]
    picks = row_count // 2
    rank = lax.broadcasted_iota(jnp.int32, (picks, 1), 0)
    place = jnp.zeros_like(rank)
    step = 1
    while step < picks:
        stride = row_count // (2 * step)
        place = jnp.where(rank >= step, (2 * (rank - step) + 1) * stride, place)
        step *= 2
    column = lax.broadcasted_iota(jnp.int32, (picks, row_count), 1)
    choose = jnp.where(place == column, 1.0, 0.0).astype(BF16)
    for plane, source in enumerate((key_ref, value_ref)):
        picked = jnp.dot(choose, source[...], preferred_element_type=F32).astype(BF16)
        for out_ref, (low, high) in zip(out_refs, cuts):
            out_ref[plane] = picked[low:high]


def pack(key_vectors, value_vectors, cuts):
    row_count, width = key_vectors.shape
    tile = width // 2
    return pl.pallas_call(
        lambda *refs: pack_kernel(*refs, cuts=cuts),
        grid=(width // tile,),
        in_specs=[pl.BlockSpec((row_count, tile), lambda j: (0, j))] * 2,
        out_specs=[
            pl.BlockSpec((2, high - low, tile), lambda j: (0, 0, j)) for low, high in cuts
        ],
        out_shape=[jax.ShapeDtypeStruct((2, high - low, width), BF16) for low, high in cuts],
        name="pack",
        compiler_params=pltpu.CompilerParams(vmem_limit_bytes=48 << 20),
        cost_estimate=pl.CostEstimate(
            flops=2 * row_count * row_count * width,
            bytes_accessed=8 * row_count * width,
            transcendentals=0,
        ),
    )(key_vectors, value_vectors)


def attend_kernel(*refs, buffers, own, first, last, low, high):
    refs = list(refs)
    query_ref = refs.pop(0)
    own_refs = [refs.pop(0), refs.pop(0)] if own else None
    packed_refs = [refs.pop(0) for _ in range(buffers)]
    bias_ref = refs.pop(0) if buffers else None
    state_in, accum_in = (None, None) if first else (refs.pop(0), refs.pop(0))
    query_count = query_ref.shape[0]
    factor = math.log2(math.e) / math.sqrt(HEAD_DIM)
    together = 2

    def one(head):
        span = pl.ds(pl.multiple_of((head + low) * HEAD_DIM, HEAD_DIM), HEAD_DIM)
        if own:
            key, value = (own_refs[0][:, span], own_refs[1][:, span])
        else:
            key = jnp.concatenate([ref[0, :, span] for ref in packed_refs], axis=0)
            value = jnp.concatenate([ref[1, :, span] for ref in packed_refs], axis=0)
        scores = lax.dot_general(
            key, query_ref[:, span], (((1,), (1,)), ((), ())), preferred_element_type=F32
        )
        if buffers:
            scores = scores + jnp.concatenate([bias_ref[...]] * (query_count // HEAD_DIM), axis=1)
        top = jnp.max(scores, axis=0, keepdims=True)
        if not first:
            state = state_in[head + low]
            top = jnp.maximum(top, state[0:1])
            shrink = jnp.exp2((state[0:1] - top) * factor)
        weights = jnp.exp2(scores * factor - top * factor)
        total = jnp.sum(weights, axis=0, keepdims=True)
        accum = jnp.dot(value.T, weights.astype(BF16), preferred_element_type=F32)
        if not first:
            total = total + shrink * state[1:2]
            accum = accum + shrink * accum_in[head + low]
        if last:
            out = pl.ds(pl.multiple_of(head * HEAD_DIM, HEAD_DIM), HEAD_DIM)
            refs[0][:, out] = (accum / total).T.astype(BF16)
        else:
            refs[0][head, 0:1, :] = top
            refs[0][head, 1:2, :] = total
            refs[1][head] = accum

    def several(step, nothing):
        for member in range(together):
            one(step * together + member)
        return nothing

    lax.fori_loop(0, (high - low) // together, several, 0)


def attend(query_vectors, own_pair, buffers, bias, carry, last, low, high, name):
    row_count = query_vectors.shape[0]
    own = own_pair is not None
    first = carry is None
    operands = [query_vectors] + (list(own_pair) if own else list(buffers) + [bias])
    operands += [] if first else list(carry)
    count = row_count if own else bias.shape[0]
    width = (high - low) * HEAD_DIM
    if last:
        shapes = [jax.ShapeDtypeStruct((row_count, width), BF16)]
    else:
        shapes = [
            jax.ShapeDtypeStruct((high - low, 8, row_count), F32),
            jax.ShapeDtypeStruct((high - low, HEAD_DIM, row_count), F32),
        ]
    held = pl.BlockSpec(memory_space=pltpu.VMEM)
    return pl.pallas_call(
        lambda *refs: attend_kernel(
            *refs, buffers=len(buffers), own=own, first=first, last=last, low=low, high=high
        ),
        in_specs=[held] * len(operands),
        out_specs=[held] * len(shapes),
        out_shape=shapes,
        name=name,
        compiler_params=pltpu.CompilerParams(vmem_limit_bytes=16 << 20),
        cost_estimate=pl.CostEstimate(
            flops=0 if own else 4 * row_count * count * width,
            bytes_accessed=0 if own else 8 * row_count * width,
            transcendentals=0 if own else row_count * count * (high - low),
        ),
    )(*operands)


def per_device(query_vectors, key_vectors, value_vectors, band_table, out_weight):
    row_count, width = query_vectors.shape
    block_count = lax.axis_size("tm")
    group_count = lax.axis_size("head")
    my_block = lax.axis_index("tm")
    my_group = lax.axis_index("head")
    table_row = lax.dynamic_index_in_dim(band_table, my_block, 0, keepdims=False)

    def move(array, block_to, group_to=lambda h: h):
        route = []
        for t in range(block_count):
            for h in range(group_count):
                to = block_to(t)
                if to is not None and 0 <= to < block_count:
                    route.append((t * group_count + h, to * group_count + group_to(h)))
        return lax.ppermute(array, AXES, route)

    def bias_of(pieces):
        blocks = jnp.stack([jnp.asarray(block, jnp.int32) for block, _, _ in pieces])
        number = np.concatenate([np.full(n, i) for i, (_, _, n) in enumerate(pieces)])
        rank = np.concatenate([np.arange(a, a + n) for _, a, n in pieces]).astype(np.int32)
        member = jnp.asarray(number[None, :] == np.arange(len(pieces))[:, None])
        here = jnp.arange(block_count, dtype=jnp.int32)[None, :] == blocks[:, None]
        band = jnp.sum(jnp.where(here, table_row[None, :], 0), axis=1)
        kept = jnp.where(jnp.any(here, axis=1), jnp.right_shift(jnp.int32(row_count), band), 0)
        limit = jnp.sum(jnp.where(member, kept[:, None], 0), axis=0)
        bias = jnp.where(jnp.asarray(rank) < limit, 0.0, MASKED).astype(F32)
        return jnp.broadcast_to(bias[:, None], (rank.size, HEAD_DIM))

    def within(block):
        return (block >= 0) & (block < block_count)

    head_count = width // HEAD_DIM
    core = lambda h: h ^ 1
    same = lambda t: t
    mine = my_group % 2
    level = my_group // 2
    out_width = out_weight.shape[1] // group_count
    away, home = (2 * (1 - level) + mine, 2 * level + mine)
    moved = move(out_weight, same, core)
    near = row_count // 2
    own_pair = (key_vectors, value_vectors)

    def further(buffers, pieces, carry, name):
        return attend(
            query_vectors, None, buffers, bias_of(pieces), carry, False, 0, head_count, name
        )

    def blocks_of(*sources):
        return [
            lax.dynamic_slice_in_dim(source, number * out_width, out_width, 1)
            for source in sources
            for number in (away, home)
        ]

    if block_count == 8:
        a, ab = (row_count // 8, row_count // 4)
        side = jnp.where(my_block % 2 == 0, 1, -1)
        far_of = lambda t: t - 2 if t % 2 == 0 else t + 2
        near_of = lambda t: t + 2 if t % 2 == 0 else t - 2
        twin_if = lambda source: lambda t: t ^ 1 if 0 <= source(t) < block_count else None
        ends = (0, 1, block_count - 2, block_count - 1)
        partner, two, opposite = (my_block ^ 1, my_block ^ 4, my_block ^ 6)
        far_block, near_block = (my_block - 2 * side, my_block + 2 * side)
        adjacent, far_cross = (my_block - side, my_block + 3 * side)
        at_end = (my_block < 2) | (my_block >= block_count - 2)
        three = jnp.where(at_end, opposite, -1)

        sent, sent_ab, sent_ba, sent_a = pack(
            key_vectors, value_vectors, [(0, near), (0, ab), (0, ab), (0, a)]
        )
        x_rows = move(sent, lambda t: t ^ 1)
        z_far = move(sent_ab, near_of)
        z_near = move(sent_ba, far_of)
        z_two = move(sent_a, lambda t: t ^ 4)
        carry = attend(query_vectors, own_pair, [], None, None, False, 0, head_count, "own")
        x_rows, z_far, z_near, z_two, state, moved = lax.optimization_barrier(
            (x_rows, z_far, z_near, z_two, carry[0], moved)
        )
        near_b = move(x_rows[:, a:ab], near_of)
        near_c = move(x_rows[:, ab:], near_of)
        cross_far = move(z_far, twin_if(far_of))
        cross_two = move(jnp.concatenate([z_near[:, :a], z_two], axis=1), lambda t: t ^ 1)
        z_three = move(z_two, lambda t: {4: 6, 5: 7, 2: 0, 3: 1}.get(t))
        carry = further(
            [x_rows, z_far, z_near, z_two],
            [(partner, 0, near), (far_block, 0, ab), (near_block, 0, ab), (two, 0, a)],
            (state, carry[1]),
            "first",
        )
        near_b, z_three, state, out_weight, moved = lax.optimization_barrier(
            (near_b, z_three, carry[0], out_weight, moved)
        )
        chain_b = move(near_b, near_of)
        cross_three = move(z_three, lambda t: t ^ 1 if t in ends else None)
        weights = blocks_of(out_weight, moved)
        near_c, state, weights = lax.optimization_barrier((near_c, state, weights))
        carry = further(
            [near_b, near_c, z_three],
            [(adjacent, a, ab - a), (adjacent, ab, near - ab), (three, 0, a)],
            (state, carry[1]),
            "middle",
        )
        buffers = [cross_far, cross_two, cross_three, chain_b]
        pieces = [
            (far_cross, 0, ab),
            (adjacent, 0, a),
            (two ^ 1, 0, a),
            (jnp.where(at_end, opposite ^ 1, -1), 0, a),
            (my_block - 3 * side, a, ab - a),
        ]
    else:
        (packed,) = pack(key_vectors, value_vectors, [(0, near)])
        received, pieces = ([], [])
        for distance in range(1, block_count):
            rows = row_count >> distance.bit_length()
            for sign in (1, -1):
                received.append(move(packed[:, :rows], lambda t: t + sign * distance))
                pieces.append((my_block - sign * distance, 0, rows))
        carry = attend(query_vectors, own_pair, [], None, None, False, 0, head_count, "own")
        carry = further([jnp.concatenate(received[:2], axis=1)], pieces[:2], carry, "first")
        buffers, pieces = ([jnp.concatenate(received[2:], axis=1)], pieces[2:])
        weights = lax.optimization_barrier(blocks_of(out_weight, moved))

    bias = bias_of(pieces)
    cut = 2 * (head_count // 4)
    parts = []
    for low, high in ((0, cut), (cut, head_count)):
        (part,) = attend(
            query_vectors, None, buffers, bias, carry, True, low, high, f"last{low}"
        )
        parts.append((part, move(part, same, core), low * HEAD_DIM, high * HEAD_DIM))

    def project(index, first, last):
        total = 0.0
        for part, other, low, high in parts:
            total = total + jnp.dot(
                part, weights[index][low:high, first:last], preferred_element_type=F32
            )
            total = total + jnp.dot(
                other, weights[index + 2][low:high, first:last], preferred_element_type=F32
            )
        return total

    half = out_width // 2
    sent = []
    for first in (0, half):
        sent.append(project(0, first, first + half).astype(BF16))
        _, held = lax.optimization_barrier((sent[-1], [part[:2] for part in parts]))
        parts = [kept + part[2:] for kept, part in zip(held, parts)]
    arrived = [move(block, same, lambda h: h ^ 2) for block in sent]
    kept, arrived[0] = lax.optimization_barrier((project(1, 0, out_width), arrived[0]))
    return (kept + jnp.concatenate(arrived, axis=1).astype(F32)).astype(BF16)


def solution(mesh):
    in_specs = (P("tm", "head"), P("tm", "head"), P("tm", "head"), P(), P("head", None))
    out_specs = P("tm", "head")
    return jax.shard_map(
        per_device, mesh=mesh, in_specs=in_specs, out_specs=out_specs, check_vma=False
    )
```

```python
import math

import jax
import jax.numpy as jnp
import numpy as np
from jax import lax
from jax.experimental import pallas as pl
from jax.experimental.pallas import tpu as pltpu
from jax.sharding import PartitionSpec as P

HEAD_DIM = 128
MASKED = -1e30
AXES = ("tm", "head")
F32 = jnp.float32
BF16 = jnp.bfloat16


def pack_kernel(key_ref, value_ref, *out_refs, cuts):
    row_count = key_ref.shape[0]
    picks = row_count // 2
    rank = lax.broadcasted_iota(jnp.int32, (picks, 1), 0)
    place = jnp.zeros_like(rank)
    step = 1
    while step < picks:
        stride = row_count // (2 * step)
        place = jnp.where(rank >= step, (2 * (rank - step) + 1) * stride, place)
        step *= 2
    column = lax.broadcasted_iota(jnp.int32, (picks, row_count), 1)
    choose = jnp.where(place == column, 1.0, 0.0).astype(BF16)
    for plane, source in enumerate((key_ref, value_ref)):
        picked = jnp.dot(choose, source[...], preferred_element_type=F32).astype(BF16)
        for out_ref, (low, high) in zip(out_refs, cuts):
            out_ref[plane] = picked[low:high]


def pack(key_vectors, value_vectors, cuts):
    row_count, width = key_vectors.shape
    tile = width // 2
    return pl.pallas_call(
        lambda *refs: pack_kernel(*refs, cuts=cuts),
        grid=(width // tile,),
        in_specs=[pl.BlockSpec((row_count, tile), lambda j: (0, j))] * 2,
        out_specs=[
            pl.BlockSpec((2, high - low, tile), lambda j: (0, 0, j)) for low, high in cuts
        ],
        out_shape=[jax.ShapeDtypeStruct((2, high - low, width), BF16) for low, high in cuts],
        name="pack",
        compiler_params=pltpu.CompilerParams(vmem_limit_bytes=48 << 20),
        cost_estimate=pl.CostEstimate(
            flops=2 * row_count * row_count * width,
            bytes_accessed=8 * row_count * width,
            transcendentals=0,
        ),
    )(key_vectors, value_vectors)


def attend_kernel(*refs, buffers, own, first, last, low, high):
    refs = list(refs)
    query_ref = refs.pop(0)
    own_refs = [refs.pop(0), refs.pop(0)] if own else None
    packed_refs = [refs.pop(0) for _ in range(buffers)]
    bias_ref = refs.pop(0) if buffers else None
    state_in, accum_in = (None, None) if first else (refs.pop(0), refs.pop(0))
    query_count = query_ref.shape[0]
    factor = math.log2(math.e) / math.sqrt(HEAD_DIM)
    together = 2

    def one(head):
        span = pl.ds(pl.multiple_of((head + low) * HEAD_DIM, HEAD_DIM), HEAD_DIM)
        if own:
            key, value = (own_refs[0][:, span], own_refs[1][:, span])
        else:
            key = jnp.concatenate([ref[0, :, span] for ref in packed_refs], axis=0)
            value = jnp.concatenate([ref[1, :, span] for ref in packed_refs], axis=0)
        scores = lax.dot_general(
            key, query_ref[:, span], (((1,), (1,)), ((), ())), preferred_element_type=F32
        )
        if buffers:
            scores = scores + jnp.concatenate([bias_ref[...]] * (query_count // HEAD_DIM), axis=1)
        top = jnp.max(scores, axis=0, keepdims=True)
        if not first:
            state = state_in[head + low]
            top = jnp.maximum(top, state[0:1])
            shrink = jnp.exp2((state[0:1] - top) * factor)
        weights = jnp.exp2(scores * factor - top * factor)
        total = jnp.sum(weights, axis=0, keepdims=True)
        accum = jnp.dot(value.T, weights.astype(BF16), preferred_element_type=F32)
        if not first:
            total = total + shrink * state[1:2]
            accum = accum + shrink * accum_in[head + low]
        if last:
            out = pl.ds(pl.multiple_of(head * HEAD_DIM, HEAD_DIM), HEAD_DIM)
            refs[0][:, out] = (accum / total).T.astype(BF16)
        else:
            refs[0][head, 0:1, :] = top
            refs[0][head, 1:2, :] = total
            refs[1][head] = accum

    def several(step, nothing):
        for member in range(together):
            one(step * together + member)
        return nothing

    lax.fori_loop(0, (high - low) // together, several, 0)


def attend(query_vectors, own_pair, buffers, bias, carry, last, low, high, name):
    row_count = query_vectors.shape[0]
    own = own_pair is not None
    first = carry is None
    operands = [query_vectors] + (list(own_pair) if own else list(buffers) + [bias])
    operands += [] if first else list(carry)
    count = row_count if own else bias.shape[0]
    width = (high - low) * HEAD_DIM
    if last:
        shapes = [jax.ShapeDtypeStruct((row_count, width), BF16)]
    else:
        shapes = [
            jax.ShapeDtypeStruct((high - low, 8, row_count), F32),
            jax.ShapeDtypeStruct((high - low, HEAD_DIM, row_count), F32),
        ]
    held = pl.BlockSpec(memory_space=pltpu.VMEM)
    return pl.pallas_call(
        lambda *refs: attend_kernel(
            *refs, buffers=len(buffers), own=own, first=first, last=last, low=low, high=high
        ),
        in_specs=[held] * len(operands),
        out_specs=[held] * len(shapes),
        out_shape=shapes,
        name=name,
        compiler_params=pltpu.CompilerParams(vmem_limit_bytes=16 << 20),
        cost_estimate=pl.CostEstimate(
            flops=0 if own else 4 * row_count * count * width,
            bytes_accessed=0 if own else 8 * row_count * width,
            transcendentals=0 if own else row_count * count * (high - low),
        ),
    )(*operands)


def per_device(query_vectors, key_vectors, value_vectors, band_table, out_weight):
    row_count, width = query_vectors.shape
    block_count = lax.axis_size("tm")
    group_count = lax.axis_size("head")
    my_block = lax.axis_index("tm")
    my_group = lax.axis_index("head")
    table_row = lax.dynamic_index_in_dim(band_table, my_block, 0, keepdims=False)

    def move(array, block_to, group_to=lambda h: h):
        route = []
        for t in range(block_count):
            for h in range(group_count):
                to = block_to(t)
                if to is not None and 0 <= to < block_count:
                    route.append((t * group_count + h, to * group_count + group_to(h)))
        return lax.ppermute(array, AXES, route)

    def bias_of(pieces):
        blocks = jnp.stack([jnp.asarray(block, jnp.int32) for block, _, _ in pieces])
        number = np.concatenate([np.full(n, i) for i, (_, _, n) in enumerate(pieces)])
        rank = np.concatenate([np.arange(a, a + n) for _, a, n in pieces]).astype(np.int32)
        member = jnp.asarray(number[None, :] == np.arange(len(pieces))[:, None])
        here = jnp.arange(block_count, dtype=jnp.int32)[None, :] == blocks[:, None]
        band = jnp.sum(jnp.where(here, table_row[None, :], 0), axis=1)
        kept = jnp.where(jnp.any(here, axis=1), jnp.right_shift(jnp.int32(row_count), band), 0)
        limit = jnp.sum(jnp.where(member, kept[:, None], 0), axis=0)
        bias = jnp.where(jnp.asarray(rank) < limit, 0.0, MASKED).astype(F32)
        return jnp.broadcast_to(bias[:, None], (rank.size, HEAD_DIM))

    def within(block):
        return (block >= 0) & (block < block_count)

    head_count = width // HEAD_DIM
    core = lambda h: h ^ 1
    same = lambda t: t
    mine = my_group % 2
    level = my_group // 2
    out_width = out_weight.shape[1] // group_count
    away, home = (2 * (1 - level) + mine, 2 * level + mine)
    moved = move(out_weight, same, core)
    near = row_count // 2
    own_pair = (key_vectors, value_vectors)

    def further(buffers, pieces, carry, name):
        return attend(
            query_vectors, None, buffers, bias_of(pieces), carry, False, 0, head_count, name
        )

    def blocks_of(*sources):
        return [
            lax.dynamic_slice_in_dim(source, number * out_width, out_width, 1)
            for source in sources
            for number in (away, home)
        ]

    if block_count == 8:
        a, ab = (row_count // 8, row_count // 4)
        side = jnp.where(my_block % 2 == 0, 1, -1)
        far_of = lambda t: t - 2 if t % 2 == 0 else t + 2
        near_of = lambda t: t + 2 if t % 2 == 0 else t - 2
        twin_if = lambda source: lambda t: t ^ 1 if 0 <= source(t) < block_count else None
        ends = (0, 1, block_count - 2, block_count - 1)
        partner, two, opposite = (my_block ^ 1, my_block ^ 4, my_block ^ 6)
        far_block, near_block = (my_block - 2 * side, my_block + 2 * side)
        adjacent, far_cross = (my_block - side, my_block + 3 * side)
        at_end = (my_block < 2) | (my_block >= block_count - 2)
        three = jnp.where(at_end, opposite, -1)

        sent, sent_ab, sent_ba, sent_a = pack(
            key_vectors, value_vectors, [(0, near), (0, ab), (0, ab), (0, a)]
        )
        x_rows = move(sent, lambda t: t ^ 1)
        z_far = move(sent_ab, near_of)
        z_near = move(sent_ba, far_of)
        z_two = move(sent_a, lambda t: t ^ 4)
        carry = attend(query_vectors, own_pair, [], None, None, False, 0, head_count, "own")
        z_far, z_near, state = lax.optimization_barrier((z_far, z_near, carry[0]))
        carry = further(
            [z_far, z_near],
            [(far_block, 0, ab), (near_block, 0, ab)],
            (state, carry[1]),
            "early",
        )
        state, out_weight, moved = lax.optimization_barrier((carry[0], out_weight, moved))
        weights = blocks_of(out_weight, moved)
        x_rows, z_near, z_two, state, weights = lax.optimization_barrier(
            (x_rows, z_near, z_two, state, weights)
        )
        near_b = move(x_rows[:, a:ab], near_of)
        near_c = move(x_rows[:, ab:], near_of)
        cross_far = move(z_far, twin_if(far_of))
        cross_two = move(jnp.concatenate([z_near[:, :a], z_two], axis=1), lambda t: t ^ 1)
        z_three = move(z_two, lambda t: {4: 6, 5: 7, 2: 0, 3: 1}.get(t))
        carry = further(
            [x_rows, z_two],
            [(partner, 0, near), (two, 0, a)],
            (state, carry[1]),
            "first",
        )
        near_b, z_three, state = lax.optimization_barrier((near_b, z_three, carry[0]))
        chain_b = move(near_b, near_of)
        cross_three = move(z_three, lambda t: t ^ 1 if t in ends else None)
        carry = further(
            [near_b, near_c, z_three, cross_far],
            [
                (adjacent, a, ab - a),
                (adjacent, ab, near - ab),
                (three, 0, a),
                (far_cross, 0, ab),
            ],
            (state, carry[1]),
            "middle",
        )
        buffers = [cross_two, cross_three, chain_b]
        pieces = [
            (adjacent, 0, a),
            (two ^ 1, 0, a),
            (jnp.where(at_end, opposite ^ 1, -1), 0, a),
            (my_block - 3 * side, a, ab - a),
        ]
    else:
        (packed,) = pack(key_vectors, value_vectors, [(0, near)])
        received, pieces = ([], [])
        for distance in range(1, block_count):
            rows = row_count >> distance.bit_length()
            for sign in (1, -1):
                received.append(move(packed[:, :rows], lambda t: t + sign * distance))
                pieces.append((my_block - sign * distance, 0, rows))
        carry = attend(query_vectors, own_pair, [], None, None, False, 0, head_count, "own")
        carry = further([jnp.concatenate(received[:2], axis=1)], pieces[:2], carry, "first")
        buffers, pieces = ([jnp.concatenate(received[2:], axis=1)], pieces[2:])
        weights = lax.optimization_barrier(blocks_of(out_weight, moved))

    bias = bias_of(pieces)
    cut = 2 * (head_count // 4)
    parts = []
    for low, high in ((0, cut), (cut, head_count)):
        (part,) = attend(
            query_vectors, None, buffers, bias, carry, True, low, high, f"last{low}"
        )
        parts.append((part, move(part, same, core), low * HEAD_DIM, high * HEAD_DIM))

    def project(index, first, last):
        total = 0.0
        for part, other, low, high in parts:
            total = total + jnp.dot(
                part, weights[index][low:high, first:last], preferred_element_type=F32
            )
            total = total + jnp.dot(
                other, weights[index + 2][low:high, first:last], preferred_element_type=F32
            )
        return total

    half = out_width // 2
    sent = []
    for first in (0, half):
        sent.append(project(0, first, first + half).astype(BF16))
        _, held = lax.optimization_barrier((sent[-1], [part[:2] for part in parts]))
        parts = [kept + part[2:] for kept, part in zip(held, parts)]
    arrived = [move(block, same, lambda h: h ^ 2) for block in sent]
    kept, arrived[0] = lax.optimization_barrier((project(1, 0, out_width), arrived[0]))
    return (kept + jnp.concatenate(arrived, axis=1).astype(F32)).astype(BF16)


def solution(mesh):
    in_specs = (P("tm", "head"), P("tm", "head"), P("tm", "head"), P(), P("head", None))
    out_specs = P("tm", "head")
    return jax.shard_map(
        per_device, mesh=mesh, in_specs=in_specs, out_specs=out_specs, check_vma=False
    )
```

```python
import math

import jax
import jax.numpy as jnp
import numpy as np
from jax import lax
from jax.experimental import pallas as pl
from jax.experimental.pallas import tpu as pltpu
from jax.sharding import PartitionSpec as P

HEAD_DIM = 128
MASKED = -1e30
AXES = ("tm", "head")
F32 = jnp.float32
BF16 = jnp.bfloat16


def pack_kernel(key_ref, value_ref, *out_refs, cuts):
    row_count = key_ref.shape[0]
    picks = row_count // 2
    rank = lax.broadcasted_iota(jnp.int32, (picks, 1), 0)
    place = jnp.zeros_like(rank)
    step = 1
    while step < picks:
        stride = row_count // (2 * step)
        place = jnp.where(rank >= step, (2 * (rank - step) + 1) * stride, place)
        step *= 2
    column = lax.broadcasted_iota(jnp.int32, (picks, row_count), 1)
    choose = jnp.where(place == column, 1.0, 0.0).astype(BF16)
    for plane, source in enumerate((key_ref, value_ref)):
        picked = jnp.dot(choose, source[...], preferred_element_type=F32).astype(BF16)
        for out_ref, (low, high) in zip(out_refs, cuts):
            out_ref[plane] = picked[low:high]


def pack(key_vectors, value_vectors, cuts):
    row_count, width = key_vectors.shape
    tile = width // 2
    return pl.pallas_call(
        lambda *refs: pack_kernel(*refs, cuts=cuts),
        grid=(width // tile,),
        in_specs=[pl.BlockSpec((row_count, tile), lambda j: (0, j))] * 2,
        out_specs=[
            pl.BlockSpec((2, high - low, tile), lambda j: (0, 0, j)) for low, high in cuts
        ],
        out_shape=[jax.ShapeDtypeStruct((2, high - low, width), BF16) for low, high in cuts],
        name="pack",
        compiler_params=pltpu.CompilerParams(vmem_limit_bytes=48 << 20),
        cost_estimate=pl.CostEstimate(
            flops=2 * row_count * row_count * width,
            bytes_accessed=8 * row_count * width,
            transcendentals=0,
        ),
    )(key_vectors, value_vectors)


def attend_kernel(*refs, buffers, own, first, last, low, high):
    refs = list(refs)
    query_ref = refs.pop(0)
    own_refs = [refs.pop(0), refs.pop(0)] if own else None
    packed_refs = [refs.pop(0) for _ in range(buffers)]
    bias_ref = refs.pop(0) if buffers else None
    state_in, accum_in = (None, None) if first else (refs.pop(0), refs.pop(0))
    query_count = query_ref.shape[0]
    factor = math.log2(math.e) / math.sqrt(HEAD_DIM)
    together = 2

    def one(head):
        span = pl.ds(pl.multiple_of((head + low) * HEAD_DIM, HEAD_DIM), HEAD_DIM)
        if own:
            key, value = (own_refs[0][:, span], own_refs[1][:, span])
        else:
            key = jnp.concatenate([ref[0, :, span] for ref in packed_refs], axis=0)
            value = jnp.concatenate([ref[1, :, span] for ref in packed_refs], axis=0)
        scores = lax.dot_general(
            key, query_ref[:, span], (((1,), (1,)), ((), ())), preferred_element_type=F32
        )
        if buffers:
            scores = scores + jnp.concatenate([bias_ref[...]] * (query_count // HEAD_DIM), axis=1)
        top = jnp.max(scores, axis=0, keepdims=True)
        if not first:
            state = state_in[head + low]
            top = jnp.maximum(top, state[0:1])
            shrink = jnp.exp2((state[0:1] - top) * factor)
        weights = jnp.exp2(scores * factor - top * factor)
        total = jnp.sum(weights, axis=0, keepdims=True)
        accum = jnp.dot(value.T, weights.astype(BF16), preferred_element_type=F32)
        if not first:
            total = total + shrink * state[1:2]
            accum = accum + shrink * accum_in[head + low]
        if last:
            out = pl.ds(pl.multiple_of(head * HEAD_DIM, HEAD_DIM), HEAD_DIM)
            refs[0][:, out] = (accum / total).T.astype(BF16)
        else:
            refs[0][head, 0:1, :] = top
            refs[0][head, 1:2, :] = total
            refs[1][head] = accum

    def several(step, nothing):
        for member in range(together):
            one(step * together + member)
        return nothing

    lax.fori_loop(0, (high - low) // together, several, 0)


def attend(query_vectors, own_pair, buffers, bias, carry, last, low, high, name):
    row_count = query_vectors.shape[0]
    own = own_pair is not None
    first = carry is None
    operands = [query_vectors] + (list(own_pair) if own else list(buffers) + [bias])
    operands += [] if first else list(carry)
    count = row_count if own else bias.shape[0]
    width = (high - low) * HEAD_DIM
    if last:
        shapes = [jax.ShapeDtypeStruct((row_count, width), BF16)]
    else:
        shapes = [
            jax.ShapeDtypeStruct((high - low, 8, row_count), F32),
            jax.ShapeDtypeStruct((high - low, HEAD_DIM, row_count), F32),
        ]
    held = pl.BlockSpec(memory_space=pltpu.VMEM)
    return pl.pallas_call(
        lambda *refs: attend_kernel(
            *refs, buffers=len(buffers), own=own, first=first, last=last, low=low, high=high
        ),
        in_specs=[held] * len(operands),
        out_specs=[held] * len(shapes),
        out_shape=shapes,
        name=name,
        compiler_params=pltpu.CompilerParams(vmem_limit_bytes=16 << 20),
        cost_estimate=pl.CostEstimate(
            flops=0 if own else 4 * row_count * count * width,
            bytes_accessed=0 if own else 8 * row_count * width,
            transcendentals=0 if own else row_count * count * (high - low),
        ),
    )(*operands)


def per_device(query_vectors, key_vectors, value_vectors, band_table, out_weight):
    row_count, width = query_vectors.shape
    block_count = lax.axis_size("tm")
    group_count = lax.axis_size("head")
    my_block = lax.axis_index("tm")
    my_group = lax.axis_index("head")
    table_row = lax.dynamic_index_in_dim(band_table, my_block, 0, keepdims=False)

    def move(array, block_to, group_to=lambda h: h):
        route = []
        for t in range(block_count):
            for h in range(group_count):
                to = block_to(t)
                if to is not None and 0 <= to < block_count:
                    route.append((t * group_count + h, to * group_count + group_to(h)))
        return lax.ppermute(array, AXES, route)

    def bias_of(pieces):
        blocks = jnp.stack([jnp.asarray(block, jnp.int32) for block, _, _ in pieces])
        number = np.concatenate([np.full(n, i) for i, (_, _, n) in enumerate(pieces)])
        rank = np.concatenate([np.arange(a, a + n) for _, a, n in pieces]).astype(np.int32)
        member = jnp.asarray(number[None, :] == np.arange(len(pieces))[:, None])
        here = jnp.arange(block_count, dtype=jnp.int32)[None, :] == blocks[:, None]
        band = jnp.sum(jnp.where(here, table_row[None, :], 0), axis=1)
        kept = jnp.where(jnp.any(here, axis=1), jnp.right_shift(jnp.int32(row_count), band), 0)
        limit = jnp.sum(jnp.where(member, kept[:, None], 0), axis=0)
        bias = jnp.where(jnp.asarray(rank) < limit, 0.0, MASKED).astype(F32)
        return jnp.broadcast_to(bias[:, None], (rank.size, HEAD_DIM))

    def within(block):
        return (block >= 0) & (block < block_count)

    head_count = width // HEAD_DIM
    core = lambda h: h ^ 1
    same = lambda t: t
    mine = my_group % 2
    level = my_group // 2
    out_width = out_weight.shape[1] // group_count
    away, home = (2 * (1 - level) + mine, 2 * level + mine)
    moved = move(out_weight, same, core)
    near = row_count // 2
    own_pair = (key_vectors, value_vectors)

    def further(buffers, pieces, carry, name):
        return attend(
            query_vectors, None, buffers, bias_of(pieces), carry, False, 0, head_count, name
        )

    def blocks_of(*sources):
        return [
            lax.dynamic_slice_in_dim(source, number * out_width, out_width, 1)
            for source in sources
            for number in (away, home)
        ]

    if block_count == 8:
        a, ab = (row_count // 8, row_count // 4)
        side = jnp.where(my_block % 2 == 0, 1, -1)
        far_of = lambda t: t - 2 if t % 2 == 0 else t + 2
        near_of = lambda t: t + 2 if t % 2 == 0 else t - 2
        twin_if = lambda source: lambda t: t ^ 1 if 0 <= source(t) < block_count else None
        ends = (0, 1, block_count - 2, block_count - 1)
        partner, two, opposite = (my_block ^ 1, my_block ^ 4, my_block ^ 6)
        far_block, near_block = (my_block - 2 * side, my_block + 2 * side)
        adjacent, far_cross = (my_block - side, my_block + 3 * side)
        at_end = (my_block < 2) | (my_block >= block_count - 2)
        three = jnp.where(at_end, opposite, -1)

        sent, sent_ab, sent_ba, sent_a = pack(
            key_vectors, value_vectors, [(0, near), (0, ab), (0, ab), (0, a)]
        )
        x_rows = move(sent, lambda t: t ^ 1)
        z_far = move(sent_ab, near_of)
        z_near = move(sent_ba, far_of)
        z_two = move(sent_a, lambda t: t ^ 4)
        carry = attend(query_vectors, own_pair, [], None, None, False, 0, head_count, "own")
        state, out_weight = lax.optimization_barrier((carry[0], out_weight))
        weights = blocks_of(out_weight)
        z_far, z_near, state, weights = lax.optimization_barrier((z_far, z_near, state, weights))
        carry = further(
            [z_far, z_near],
            [(far_block, 0, ab), (near_block, 0, ab)],
            (state, carry[1]),
            "early",
        )
        state, moved = lax.optimization_barrier((carry[0], moved))
        weights = weights + blocks_of(moved)
        x_rows, z_near, z_two, state, weights = lax.optimization_barrier(
            (x_rows, z_near, z_two, state, weights)
        )
        near_b = move(x_rows[:, a:ab], near_of)
        near_c = move(x_rows[:, ab:], near_of)
        cross_far = move(z_far, twin_if(far_of))
        cross_two = move(jnp.concatenate([z_near[:, :a], z_two], axis=1), lambda t: t ^ 1)
        z_three = move(z_two, lambda t: {4: 6, 5: 7, 2: 0, 3: 1}.get(t))
        carry = further(
            [x_rows, z_two],
            [(partner, 0, near), (two, 0, a)],
            (state, carry[1]),
            "first",
        )
        near_b, z_three, state = lax.optimization_barrier((near_b, z_three, carry[0]))
        chain_b = move(near_b, near_of)
        cross_three = move(z_three, lambda t: t ^ 1 if t in ends else None)
        carry = further(
            [near_b, near_c, z_three, cross_far],
            [
                (adjacent, a, ab - a),
                (adjacent, ab, near - ab),
                (three, 0, a),
                (far_cross, 0, ab),
            ],
            (state, carry[1]),
            "middle",
        )
        buffers = [cross_two, cross_three, chain_b]
        pieces = [
            (adjacent, 0, a),
            (two ^ 1, 0, a),
            (jnp.where(at_end, opposite ^ 1, -1), 0, a),
            (my_block - 3 * side, a, ab - a),
        ]
    else:
        (packed,) = pack(key_vectors, value_vectors, [(0, near)])
        received, pieces = ([], [])
        for distance in range(1, block_count):
            rows = row_count >> distance.bit_length()
            for sign in (1, -1):
                received.append(move(packed[:, :rows], lambda t: t + sign * distance))
                pieces.append((my_block - sign * distance, 0, rows))
        carry = attend(query_vectors, own_pair, [], None, None, False, 0, head_count, "own")
        carry = further([jnp.concatenate(received[:2], axis=1)], pieces[:2], carry, "first")
        buffers, pieces = ([jnp.concatenate(received[2:], axis=1)], pieces[2:])
        weights = lax.optimization_barrier(blocks_of(out_weight, moved))

    bias = bias_of(pieces)
    cut = 2 * (head_count // 4)
    parts = []
    for low, high in ((0, cut), (cut, head_count)):
        (part,) = attend(
            query_vectors, None, buffers, bias, carry, True, low, high, f"last{low}"
        )
        parts.append((part, move(part, same, core), low * HEAD_DIM, high * HEAD_DIM))

    def project(index, first, last):
        total = 0.0
        for part, other, low, high in parts:
            total = total + jnp.dot(
                part, weights[index][low:high, first:last], preferred_element_type=F32
            )
            total = total + jnp.dot(
                other, weights[index + 2][low:high, first:last], preferred_element_type=F32
            )
        return total

    half = out_width // 2
    sent = []
    for first in (0, half):
        sent.append(project(0, first, first + half).astype(BF16))
        _, held = lax.optimization_barrier((sent[-1], [part[:2] for part in parts]))
        parts = [kept + part[2:] for kept, part in zip(held, parts)]
    arrived = [move(block, same, lambda h: h ^ 2) for block in sent]
    kept, arrived[0] = lax.optimization_barrier((project(1, 0, out_width), arrived[0]))
    return (kept + jnp.concatenate(arrived, axis=1).astype(F32)).astype(BF16)


def solution(mesh):
    in_specs = (P("tm", "head"), P("tm", "head"), P("tm", "head"), P(), P("head", None))
    out_specs = P("tm", "head")
    return jax.shard_map(
        per_device, mesh=mesh, in_specs=in_specs, out_specs=out_specs, check_vma=False
    )
```

```python
import math

import jax
import jax.numpy as jnp
import numpy as np
from jax import lax
from jax.experimental import pallas as pl
from jax.experimental.pallas import tpu as pltpu
from jax.sharding import PartitionSpec as P

HEAD_DIM = 128
MASKED = -1e30
AXES = ("tm", "head")
F32 = jnp.float32
BF16 = jnp.bfloat16


def pack_kernel(key_ref, value_ref, *out_refs, cuts):
    row_count = key_ref.shape[0]
    picks = row_count // 2
    rank = lax.broadcasted_iota(jnp.int32, (picks, 1), 0)
    place = jnp.zeros_like(rank)
    step = 1
    while step < picks:
        stride = row_count // (2 * step)
        place = jnp.where(rank >= step, (2 * (rank - step) + 1) * stride, place)
        step *= 2
    column = lax.broadcasted_iota(jnp.int32, (picks, row_count), 1)
    choose = jnp.where(place == column, 1.0, 0.0).astype(BF16)
    for plane, source in enumerate((key_ref, value_ref)):
        picked = jnp.dot(choose, source[...], preferred_element_type=F32).astype(BF16)
        for out_ref, (low, high) in zip(out_refs, cuts):
            out_ref[plane] = picked[low:high]


def pack(key_vectors, value_vectors, cuts):
    row_count, width = key_vectors.shape
    tile = width // 2
    return pl.pallas_call(
        lambda *refs: pack_kernel(*refs, cuts=cuts),
        grid=(width // tile,),
        in_specs=[pl.BlockSpec((row_count, tile), lambda j: (0, j))] * 2,
        out_specs=[
            pl.BlockSpec((2, high - low, tile), lambda j: (0, 0, j)) for low, high in cuts
        ],
        out_shape=[jax.ShapeDtypeStruct((2, high - low, width), BF16) for low, high in cuts],
        name="pack",
        compiler_params=pltpu.CompilerParams(vmem_limit_bytes=48 << 20),
        cost_estimate=pl.CostEstimate(
            flops=2 * row_count * row_count * width,
            bytes_accessed=8 * row_count * width,
            transcendentals=0,
        ),
    )(key_vectors, value_vectors)


def attend_kernel(*refs, buffers, own, first, last, low, high):
    refs = list(refs)
    query_ref = refs.pop(0)
    own_refs = [refs.pop(0), refs.pop(0)] if own else None
    packed_refs = [refs.pop(0) for _ in range(buffers)]
    bias_ref = refs.pop(0) if buffers else None
    state_in, accum_in = (None, None) if first else (refs.pop(0), refs.pop(0))
    query_count = query_ref.shape[0]
    factor = math.log2(math.e) / math.sqrt(HEAD_DIM)
    together = 2

    def one(head):
        span = pl.ds(pl.multiple_of((head + low) * HEAD_DIM, HEAD_DIM), HEAD_DIM)
        if own:
            key, value = (own_refs[0][:, span], own_refs[1][:, span])
        else:
            key = jnp.concatenate([ref[0, :, span] for ref in packed_refs], axis=0)
            value = jnp.concatenate([ref[1, :, span] for ref in packed_refs], axis=0)
        scores = lax.dot_general(
            key, query_ref[:, span], (((1,), (1,)), ((), ())), preferred_element_type=F32
        )
        if buffers:
            scores = scores + jnp.concatenate([bias_ref[...]] * (query_count // HEAD_DIM), axis=1)
        top = jnp.max(scores, axis=0, keepdims=True)
        if not first:
            state = state_in[head + low]
            top = jnp.maximum(top, state[0:1])
            shrink = jnp.exp2((state[0:1] - top) * factor)
        weights = jnp.exp2(scores * factor - top * factor)
        total = jnp.sum(weights, axis=0, keepdims=True)
        accum = jnp.dot(value.T, weights.astype(BF16), preferred_element_type=F32)
        if not first:
            total = total + shrink * state[1:2]
            accum = accum + shrink * accum_in[head + low]
        if last:
            out = pl.ds(pl.multiple_of(head * HEAD_DIM, HEAD_DIM), HEAD_DIM)
            refs[0][:, out] = (accum / total).T.astype(BF16)
        else:
            refs[0][head, 0:1, :] = top
            refs[0][head, 1:2, :] = total
            refs[1][head] = accum

    def several(step, nothing):
        for member in range(together):
            one(step * together + member)
        return nothing

    lax.fori_loop(0, (high - low) // together, several, 0)


def attend(query_vectors, own_pair, buffers, bias, carry, last, low, high, name):
    row_count = query_vectors.shape[0]
    own = own_pair is not None
    first = carry is None
    operands = [query_vectors] + (list(own_pair) if own else list(buffers) + [bias])
    operands += [] if first else list(carry)
    count = row_count if own else bias.shape[0]
    width = (high - low) * HEAD_DIM
    if last:
        shapes = [jax.ShapeDtypeStruct((row_count, width), BF16)]
    else:
        shapes = [
            jax.ShapeDtypeStruct((high - low, 8, row_count), F32),
            jax.ShapeDtypeStruct((high - low, HEAD_DIM, row_count), F32),
        ]
    held = pl.BlockSpec(memory_space=pltpu.VMEM)
    scale = {"own": 0, "early": 1, "first": 1}.get(name, 1)
    return pl.pallas_call(
        lambda *refs: attend_kernel(
            *refs, buffers=len(buffers), own=own, first=first, last=last, low=low, high=high
        ),
        in_specs=[held] * len(operands),
        out_specs=[held] * len(shapes),
        out_shape=shapes,
        name=name,
        compiler_params=pltpu.CompilerParams(vmem_limit_bytes=16 << 20),
        cost_estimate=pl.CostEstimate(
            flops=scale * 4 * row_count * count * width,
            bytes_accessed=scale * 8 * row_count * width,
            transcendentals=scale * row_count * count * (high - low),
        ),
    )(*operands)


def per_device(query_vectors, key_vectors, value_vectors, band_table, out_weight):
    row_count, width = query_vectors.shape
    block_count = lax.axis_size("tm")
    group_count = lax.axis_size("head")
    my_block = lax.axis_index("tm")
    my_group = lax.axis_index("head")
    table_row = lax.dynamic_index_in_dim(band_table, my_block, 0, keepdims=False)

    def move(array, block_to, group_to=lambda h: h):
        route = []
        for t in range(block_count):
            for h in range(group_count):
                to = block_to(t)
                if to is not None and 0 <= to < block_count:
                    route.append((t * group_count + h, to * group_count + group_to(h)))
        return lax.ppermute(array, AXES, route)

    def bias_of(pieces):
        blocks = jnp.stack([jnp.asarray(block, jnp.int32) for block, _, _ in pieces])
        number = np.concatenate([np.full(n, i) for i, (_, _, n) in enumerate(pieces)])
        rank = np.concatenate([np.arange(a, a + n) for _, a, n in pieces]).astype(np.int32)
        member = jnp.asarray(number[None, :] == np.arange(len(pieces))[:, None])
        here = jnp.arange(block_count, dtype=jnp.int32)[None, :] == blocks[:, None]
        band = jnp.sum(jnp.where(here, table_row[None, :], 0), axis=1)
        kept = jnp.where(jnp.any(here, axis=1), jnp.right_shift(jnp.int32(row_count), band), 0)
        limit = jnp.sum(jnp.where(member, kept[:, None], 0), axis=0)
        bias = jnp.where(jnp.asarray(rank) < limit, 0.0, MASKED).astype(F32)
        return jnp.broadcast_to(bias[:, None], (rank.size, HEAD_DIM))

    def within(block):
        return (block >= 0) & (block < block_count)

    head_count = width // HEAD_DIM
    core = lambda h: h ^ 1
    same = lambda t: t
    mine = my_group % 2
    level = my_group // 2
    out_width = out_weight.shape[1] // group_count
    away, home = (2 * (1 - level) + mine, 2 * level + mine)
    moved = move(out_weight, same, core)
    near = row_count // 2
    own_pair = (key_vectors, value_vectors)

    def further(buffers, pieces, carry, name):
        return attend(
            query_vectors, None, buffers, bias_of(pieces), carry, False, 0, head_count, name
        )

    def blocks_of(*sources):
        return [
            lax.dynamic_slice_in_dim(source, number * out_width, out_width, 1)
            for source in sources
            for number in (away, home)
        ]

    if block_count == 8:
        a, ab = (row_count // 8, row_count // 4)
        side = jnp.where(my_block % 2 == 0, 1, -1)
        far_of = lambda t: t - 2 if t % 2 == 0 else t + 2
        near_of = lambda t: t + 2 if t % 2 == 0 else t - 2
        twin_if = lambda source: lambda t: t ^ 1 if 0 <= source(t) < block_count else None
        ends = (0, 1, block_count - 2, block_count - 1)
        partner, two, opposite = (my_block ^ 1, my_block ^ 4, my_block ^ 6)
        far_block, near_block = (my_block - 2 * side, my_block + 2 * side)
        adjacent, far_cross = (my_block - side, my_block + 3 * side)
        at_end = (my_block < 2) | (my_block >= block_count - 2)
        three = jnp.where(at_end, opposite, -1)

        sent, sent_ab, sent_ba, sent_a = pack(
            key_vectors, value_vectors, [(0, near), (0, ab), (0, ab), (0, a)]
        )
        x_rows = move(sent, lambda t: t ^ 1)
        z_far = move(sent_ab, near_of)
        z_near = move(sent_ba, far_of)
        z_two = move(sent_a, lambda t: t ^ 4)
        carry = attend(query_vectors, own_pair, [], None, None, False, 0, head_count, "own")
        state, out_weight = lax.optimization_barrier((carry[0], out_weight))
        weights = blocks_of(out_weight)
        z_far, z_near, state, weights = lax.optimization_barrier((z_far, z_near, state, weights))
        carry = further(
            [z_far, z_near],
            [(far_block, 0, ab), (near_block, 0, ab)],
            (state, carry[1]),
            "early",
        )
        x_rows, z_near, z_two, state, weights, moved = lax.optimization_barrier(
            (x_rows, z_near, z_two, carry[0], weights, moved)
        )
        near_b = move(x_rows[:, a:ab], near_of)
        near_c = move(x_rows[:, ab:], near_of)
        cross_far = move(z_far, twin_if(far_of))
        cross_two = move(jnp.concatenate([z_near[:, :a], z_two], axis=1), lambda t: t ^ 1)
        z_three = move(z_two, lambda t: {4: 6, 5: 7, 2: 0, 3: 1}.get(t))
        carry = further(
            [x_rows, z_two],
            [(partner, 0, near), (two, 0, a)],
            (state, carry[1]),
            "first",
        )
        near_b, z_three, state, moved = lax.optimization_barrier(
            (near_b, z_three, carry[0], moved)
        )
        weights = weights + blocks_of(moved)
        chain_b = move(near_b, near_of)
        cross_three = move(z_three, lambda t: t ^ 1 if t in ends else None)
        near_c, state, weights = lax.optimization_barrier((near_c, state, weights))
        carry = further(
            [near_b, near_c, z_three, cross_far],
            [
                (adjacent, a, ab - a),
                (adjacent, ab, near - ab),
                (three, 0, a),
                (far_cross, 0, ab),
            ],
            (state, carry[1]),
            "middle",
        )
        buffers = [cross_two, cross_three, chain_b]
        pieces = [
            (adjacent, 0, a),
            (two ^ 1, 0, a),
            (jnp.where(at_end, opposite ^ 1, -1), 0, a),
            (my_block - 3 * side, a, ab - a),
        ]
    else:
        (packed,) = pack(key_vectors, value_vectors, [(0, near)])
        received, pieces = ([], [])
        for distance in range(1, block_count):
            rows = row_count >> distance.bit_length()
            for sign in (1, -1):
                received.append(move(packed[:, :rows], lambda t: t + sign * distance))
                pieces.append((my_block - sign * distance, 0, rows))
        carry = attend(query_vectors, own_pair, [], None, None, False, 0, head_count, "own")
        carry = further([jnp.concatenate(received[:2], axis=1)], pieces[:2], carry, "first")
        buffers, pieces = ([jnp.concatenate(received[2:], axis=1)], pieces[2:])
        weights = lax.optimization_barrier(blocks_of(out_weight, moved))

    bias = bias_of(pieces)
    cut = 2 * (head_count // 4)
    parts = []
    for low, high in ((0, cut), (cut, head_count)):
        (part,) = attend(
            query_vectors, None, buffers, bias, carry, True, low, high, f"last{low}"
        )
        parts.append((part, move(part, same, core), low * HEAD_DIM, high * HEAD_DIM))

    def project(index, first, last):
        total = 0.0
        for part, other, low, high in parts:
            total = total + jnp.dot(
                part, weights[index][low:high, first:last], preferred_element_type=F32
            )
            total = total + jnp.dot(
                other, weights[index + 2][low:high, first:last], preferred_element_type=F32
            )
        return total

    half = out_width // 2
    sent = []
    for first in (0, half):
        sent.append(project(0, first, first + half).astype(BF16))
        _, held = lax.optimization_barrier((sent[-1], [part[:2] for part in parts]))
        parts = [kept + part[2:] for kept, part in zip(held, parts)]
    arrived = [move(block, same, lambda h: h ^ 2) for block in sent]
    kept, arrived[0] = lax.optimization_barrier((project(1, 0, out_width), arrived[0]))
    return (kept + jnp.concatenate(arrived, axis=1).astype(F32)).astype(BF16)


def solution(mesh):
    in_specs = (P("tm", "head"), P("tm", "head"), P("tm", "head"), P(), P("head", None))
    out_specs = P("tm", "head")
    return jax.shard_map(
        per_device, mesh=mesh, in_specs=in_specs, out_specs=out_specs, check_vma=False
    )
```

```python
import math

import jax
import jax.numpy as jnp
import numpy as np
from jax import lax
from jax.experimental import pallas as pl
from jax.experimental.pallas import tpu as pltpu
from jax.sharding import PartitionSpec as P

HEAD_DIM = 128
MASKED = -1e30
AXES = ("tm", "head")
F32 = jnp.float32
BF16 = jnp.bfloat16


def pack_kernel(key_ref, value_ref, *out_refs, cuts):
    row_count = key_ref.shape[0]
    picks = row_count // 2
    rank = lax.broadcasted_iota(jnp.int32, (picks, 1), 0)
    place = jnp.zeros_like(rank)
    step = 1
    while step < picks:
        stride = row_count // (2 * step)
        place = jnp.where(rank >= step, (2 * (rank - step) + 1) * stride, place)
        step *= 2
    column = lax.broadcasted_iota(jnp.int32, (picks, row_count), 1)
    choose = jnp.where(place == column, 1.0, 0.0).astype(BF16)
    for plane, source in enumerate((key_ref, value_ref)):
        picked = jnp.dot(choose, source[...], preferred_element_type=F32).astype(BF16)
        for out_ref, (low, high) in zip(out_refs, cuts):
            out_ref[plane] = picked[low:high]


def pack(key_vectors, value_vectors, cuts):
    row_count, width = key_vectors.shape
    tile = width // 2
    return pl.pallas_call(
        lambda *refs: pack_kernel(*refs, cuts=cuts),
        grid=(width // tile,),
        in_specs=[pl.BlockSpec((row_count, tile), lambda j: (0, j))] * 2,
        out_specs=[
            pl.BlockSpec((2, high - low, tile), lambda j: (0, 0, j)) for low, high in cuts
        ],
        out_shape=[jax.ShapeDtypeStruct((2, high - low, width), BF16) for low, high in cuts],
        name="pack",
        compiler_params=pltpu.CompilerParams(vmem_limit_bytes=48 << 20),
        cost_estimate=pl.CostEstimate(
            flops=2 * row_count * row_count * width,
            bytes_accessed=8 * row_count * width,
            transcendentals=0,
        ),
    )(key_vectors, value_vectors)


def attend_kernel(*refs, buffers, own, first, last, low, high):
    refs = list(refs)
    query_ref = refs.pop(0)
    own_refs = [refs.pop(0), refs.pop(0)] if own else None
    packed_refs = [refs.pop(0) for _ in range(buffers)]
    bias_ref = refs.pop(0) if buffers else None
    state_in, accum_in = (None, None) if first else (refs.pop(0), refs.pop(0))
    query_count = query_ref.shape[0]
    factor = math.log2(math.e) / math.sqrt(HEAD_DIM)
    together = 2

    def one(head):
        span = pl.ds(pl.multiple_of((head + low) * HEAD_DIM, HEAD_DIM), HEAD_DIM)
        if own:
            key, value = (own_refs[0][:, span], own_refs[1][:, span])
        else:
            key = jnp.concatenate([ref[0, :, span] for ref in packed_refs], axis=0)
            value = jnp.concatenate([ref[1, :, span] for ref in packed_refs], axis=0)
        scores = lax.dot_general(
            key, query_ref[:, span], (((1,), (1,)), ((), ())), preferred_element_type=F32
        )
        if buffers:
            scores = scores + jnp.concatenate([bias_ref[...]] * (query_count // HEAD_DIM), axis=1)
        top = jnp.max(scores, axis=0, keepdims=True)
        if not first:
            state = state_in[head + low]
            top = jnp.maximum(top, state[0:1])
            shrink = jnp.exp2((state[0:1] - top) * factor)
        weights = jnp.exp2(scores * factor - top * factor)
        total = jnp.sum(weights, axis=0, keepdims=True)
        accum = jnp.dot(value.T, weights.astype(BF16), preferred_element_type=F32)
        if not first:
            total = total + shrink * state[1:2]
            accum = accum + shrink * accum_in[head + low]
        if last:
            out = pl.ds(pl.multiple_of(head * HEAD_DIM, HEAD_DIM), HEAD_DIM)
            refs[0][:, out] = (accum / total).T.astype(BF16)
        else:
            refs[0][head, 0:1, :] = top
            refs[0][head, 1:2, :] = total
            refs[1][head] = accum

    def several(step, nothing):
        for member in range(together):
            one(step * together + member)
        return nothing

    lax.fori_loop(0, (high - low) // together, several, 0)


def attend(query_vectors, own_pair, buffers, bias, carry, last, low, high, name):
    row_count = query_vectors.shape[0]
    own = own_pair is not None
    first = carry is None
    operands = [query_vectors] + (list(own_pair) if own else list(buffers) + [bias])
    operands += [] if first else list(carry)
    count = row_count if own else bias.shape[0]
    width = (high - low) * HEAD_DIM
    if last:
        shapes = [jax.ShapeDtypeStruct((row_count, width), BF16)]
    else:
        shapes = [
            jax.ShapeDtypeStruct((high - low, 8, row_count), F32),
            jax.ShapeDtypeStruct((high - low, HEAD_DIM, row_count), F32),
        ]
    held = pl.BlockSpec(memory_space=pltpu.VMEM)
    scale = {"own": 0, "early": 1, "first": 1}.get(name, 1)
    return pl.pallas_call(
        lambda *refs: attend_kernel(
            *refs, buffers=len(buffers), own=own, first=first, last=last, low=low, high=high
        ),
        in_specs=[held] * len(operands),
        out_specs=[held] * len(shapes),
        out_shape=shapes,
        name=name,
        compiler_params=pltpu.CompilerParams(vmem_limit_bytes=16 << 20),
        cost_estimate=pl.CostEstimate(
            flops=scale * 4 * row_count * count * width,
            bytes_accessed=scale * 8 * row_count * width,
            transcendentals=scale * row_count * count * (high - low),
        ),
    )(*operands)


def per_device(query_vectors, key_vectors, value_vectors, band_table, out_weight):
    row_count, width = query_vectors.shape
    block_count = lax.axis_size("tm")
    group_count = lax.axis_size("head")
    my_block = lax.axis_index("tm")
    my_group = lax.axis_index("head")
    table_row = lax.dynamic_index_in_dim(band_table, my_block, 0, keepdims=False)

    def move(array, block_to, group_to=lambda h: h):
        route = []
        for t in range(block_count):
            for h in range(group_count):
                to = block_to(t)
                if to is not None and 0 <= to < block_count:
                    route.append((t * group_count + h, to * group_count + group_to(h)))
        return lax.ppermute(array, AXES, route)

    def bias_of(pieces):
        blocks = jnp.stack([jnp.asarray(block, jnp.int32) for block, _, _ in pieces])
        number = np.concatenate([np.full(n, i) for i, (_, _, n) in enumerate(pieces)])
        rank = np.concatenate([np.arange(a, a + n) for _, a, n in pieces]).astype(np.int32)
        member = jnp.asarray(number[None, :] == np.arange(len(pieces))[:, None])
        here = jnp.arange(block_count, dtype=jnp.int32)[None, :] == blocks[:, None]
        band = jnp.sum(jnp.where(here, table_row[None, :], 0), axis=1)
        kept = jnp.where(jnp.any(here, axis=1), jnp.right_shift(jnp.int32(row_count), band), 0)
        limit = jnp.sum(jnp.where(member, kept[:, None], 0), axis=0)
        bias = jnp.where(jnp.asarray(rank) < limit, 0.0, MASKED).astype(F32)
        return jnp.broadcast_to(bias[:, None], (rank.size, HEAD_DIM))

    def within(block):
        return (block >= 0) & (block < block_count)

    head_count = width // HEAD_DIM
    core = lambda h: h ^ 1
    same = lambda t: t
    mine = my_group % 2
    level = my_group // 2
    out_width = out_weight.shape[1] // group_count
    away, home = (2 * (1 - level) + mine, 2 * level + mine)
    moved = move(out_weight, same, core)
    near = row_count // 2
    own_pair = (key_vectors, value_vectors)

    def further(buffers, pieces, carry, name):
        return attend(
            query_vectors, None, buffers, bias_of(pieces), carry, False, 0, head_count, name
        )

    def blocks_of(*sources):
        return [
            lax.dynamic_slice_in_dim(source, number * out_width, out_width, 1)
            for source in sources
            for number in (away, home)
        ]

    if block_count == 8:
        a, ab = (row_count // 8, row_count // 4)
        side = jnp.where(my_block % 2 == 0, 1, -1)
        far_of = lambda t: t - 2 if t % 2 == 0 else t + 2
        near_of = lambda t: t + 2 if t % 2 == 0 else t - 2
        twin_if = lambda source: lambda t: t ^ 1 if 0 <= source(t) < block_count else None
        ends = (0, 1, block_count - 2, block_count - 1)
        partner, two, opposite = (my_block ^ 1, my_block ^ 4, my_block ^ 6)
        far_block, near_block = (my_block - 2 * side, my_block + 2 * side)
        adjacent, far_cross = (my_block - side, my_block + 3 * side)
        at_end = (my_block < 2) | (my_block >= block_count - 2)
        three = jnp.where(at_end, opposite, -1)

        sent, sent_ab, sent_ba, sent_a = pack(
            key_vectors, value_vectors, [(0, near), (0, ab), (0, ab), (0, a)]
        )
        x_rows = move(sent, lambda t: t ^ 1)
        z_far = move(sent_ab, near_of)
        z_near = move(sent_ba, far_of)
        z_two = move(sent_a, lambda t: t ^ 4)
        carry = attend(query_vectors, own_pair, [], None, None, False, 0, head_count, "own")
        state, out_weight = lax.optimization_barrier((carry[0], out_weight))
        weights = blocks_of(out_weight)
        z_far, z_near, state, weights = lax.optimization_barrier((z_far, z_near, state, weights))
        carry = further(
            [z_far, z_near],
            [(far_block, 0, ab), (near_block, 0, ab)],
            (state, carry[1]),
            "early",
        )
        x_rows, z_near, z_two, state, weights, moved = lax.optimization_barrier(
            (x_rows, z_near, z_two, carry[0], weights, moved)
        )
        near_b = move(x_rows[:, a:ab], near_of)
        near_c = move(x_rows[:, ab:], near_of)
        cross_far = move(z_far, twin_if(far_of))
        cross_two = move(jnp.concatenate([z_near[:, :a], z_two], axis=1), lambda t: t ^ 1)
        z_three = move(z_two, lambda t: {4: 6, 5: 7, 2: 0, 3: 1}.get(t))
        carry = further(
            [x_rows, z_two],
            [(partner, 0, near), (two, 0, a)],
            (state, carry[1]),
            "first",
        )
        near_b, z_three, state, moved = lax.optimization_barrier(
            (near_b, z_three, carry[0], moved)
        )
        weights = weights + blocks_of(moved)
        chain_b = move(near_b, near_of)
        cross_three = move(z_three, lambda t: t ^ 1 if t in ends else None)
        state, weights = lax.optimization_barrier((state, weights))
        carry = further(
            [near_b, z_three, cross_far, cross_two],
            [
                (adjacent, a, ab - a),
                (three, 0, a),
                (far_cross, 0, ab),
                (adjacent, 0, a),
                (two ^ 1, 0, a),
            ],
            (state, carry[1]),
            "middle",
        )
        buffers = [near_c, cross_three, chain_b]
        pieces = [
            (adjacent, ab, near - ab),
            (jnp.where(at_end, opposite ^ 1, -1), 0, a),
            (my_block - 3 * side, a, ab - a),
        ]
    else:
        (packed,) = pack(key_vectors, value_vectors, [(0, near)])
        received, pieces = ([], [])
        for distance in range(1, block_count):
            rows = row_count >> distance.bit_length()
            for sign in (1, -1):
                received.append(move(packed[:, :rows], lambda t: t + sign * distance))
                pieces.append((my_block - sign * distance, 0, rows))
        carry = attend(query_vectors, own_pair, [], None, None, False, 0, head_count, "own")
        carry = further([jnp.concatenate(received[:2], axis=1)], pieces[:2], carry, "first")
        buffers, pieces = ([jnp.concatenate(received[2:], axis=1)], pieces[2:])
        weights = lax.optimization_barrier(blocks_of(out_weight, moved))

    bias = bias_of(pieces)
    cut = 2 * (head_count // 4)
    parts = []
    for low, high in ((0, cut), (cut, head_count)):
        (part,) = attend(
            query_vectors, None, buffers, bias, carry, True, low, high, f"last{low}"
        )
        parts.append((part, move(part, same, core), low * HEAD_DIM, high * HEAD_DIM))

    def project(index, first, last):
        total = 0.0
        for part, other, low, high in parts:
            total = total + jnp.dot(
                part, weights[index][low:high, first:last], preferred_element_type=F32
            )
            total = total + jnp.dot(
                other, weights[index + 2][low:high, first:last], preferred_element_type=F32
            )
        return total

    half = out_width // 2
    sent = []
    for first in (0, half):
        sent.append(project(0, first, first + half).astype(BF16))
        _, held = lax.optimization_barrier((sent[-1], [part[:2] for part in parts]))
        parts = [kept + part[2:] for kept, part in zip(held, parts)]
    arrived = [move(block, same, lambda h: h ^ 2) for block in sent]
    kept, arrived[0] = lax.optimization_barrier((project(1, 0, out_width), arrived[0]))
    return (kept + jnp.concatenate(arrived, axis=1).astype(F32)).astype(BF16)


def solution(mesh):
    in_specs = (P("tm", "head"), P("tm", "head"), P("tm", "head"), P(), P("head", None))
    out_specs = P("tm", "head")
    return jax.shard_map(
        per_device, mesh=mesh, in_specs=in_specs, out_specs=out_specs, check_vma=False
    )
```

```python
import math

import jax
import jax.numpy as jnp
import numpy as np
from jax import lax
from jax.experimental import pallas as pl
from jax.experimental.pallas import tpu as pltpu
from jax.sharding import PartitionSpec as P

HEAD_DIM = 128
MASKED = -1e30
AXES = ("tm", "head")
F32 = jnp.float32
BF16 = jnp.bfloat16


def pack_kernel(key_ref, value_ref, *out_refs, cuts):
    row_count = key_ref.shape[0]
    picks = row_count // 2
    rank = lax.broadcasted_iota(jnp.int32, (picks, 1), 0)
    place = jnp.zeros_like(rank)
    step = 1
    while step < picks:
        stride = row_count // (2 * step)
        place = jnp.where(rank >= step, (2 * (rank - step) + 1) * stride, place)
        step *= 2
    column = lax.broadcasted_iota(jnp.int32, (picks, row_count), 1)
    choose = jnp.where(place == column, 1.0, 0.0).astype(BF16)
    for plane, source in enumerate((key_ref, value_ref)):
        picked = jnp.dot(choose, source[...], preferred_element_type=F32).astype(BF16)
        for out_ref, (low, high) in zip(out_refs, cuts):
            out_ref[plane] = picked[low:high]


def pack(key_vectors, value_vectors, cuts):
    row_count, width = key_vectors.shape
    tile = width // 2
    return pl.pallas_call(
        lambda *refs: pack_kernel(*refs, cuts=cuts),
        grid=(width // tile,),
        in_specs=[pl.BlockSpec((row_count, tile), lambda j: (0, j))] * 2,
        out_specs=[
            pl.BlockSpec((2, high - low, tile), lambda j: (0, 0, j)) for low, high in cuts
        ],
        out_shape=[jax.ShapeDtypeStruct((2, high - low, width), BF16) for low, high in cuts],
        name="pack",
        compiler_params=pltpu.CompilerParams(vmem_limit_bytes=48 << 20),
        cost_estimate=pl.CostEstimate(
            flops=2 * row_count * row_count * width,
            bytes_accessed=8 * row_count * width,
            transcendentals=0,
        ),
    )(key_vectors, value_vectors)


def attend_kernel(*refs, buffers, own, first, last, low, high):
    refs = list(refs)
    query_ref = refs.pop(0)
    own_refs = [refs.pop(0), refs.pop(0)] if own else None
    packed_refs = [refs.pop(0) for _ in range(buffers)]
    bias_ref = refs.pop(0) if buffers else None
    state_in, accum_in = (None, None) if first else (refs.pop(0), refs.pop(0))
    query_count = query_ref.shape[0]
    factor = math.log2(math.e) / math.sqrt(HEAD_DIM)
    together = 2

    def one(head):
        span = pl.ds(pl.multiple_of((head + low) * HEAD_DIM, HEAD_DIM), HEAD_DIM)
        if own:
            key, value = (own_refs[0][:, span], own_refs[1][:, span])
        else:
            key = jnp.concatenate([ref[0, :, span] for ref in packed_refs], axis=0)
            value = jnp.concatenate([ref[1, :, span] for ref in packed_refs], axis=0)
        scores = lax.dot_general(
            key, query_ref[:, span], (((1,), (1,)), ((), ())), preferred_element_type=F32
        )
        if buffers:
            scores = scores + jnp.concatenate([bias_ref[...]] * (query_count // HEAD_DIM), axis=1)
        top = jnp.max(scores, axis=0, keepdims=True)
        if not first:
            state = state_in[head + low]
            top = jnp.maximum(top, state[0:1])
            shrink = jnp.exp2((state[0:1] - top) * factor)
        weights = jnp.exp2(scores * factor - top * factor)
        total = jnp.sum(weights, axis=0, keepdims=True)
        accum = jnp.dot(value.T, weights.astype(BF16), preferred_element_type=F32)
        if not first:
            total = total + shrink * state[1:2]
            accum = accum + shrink * accum_in[head + low]
        if last:
            out = pl.ds(pl.multiple_of(head * HEAD_DIM, HEAD_DIM), HEAD_DIM)
            refs[0][:, out] = (accum / total).T.astype(BF16)
        else:
            refs[0][head, 0:1, :] = top
            refs[0][head, 1:2, :] = total
            refs[1][head] = accum

    def several(step, nothing):
        for member in range(together):
            one(step * together + member)
        return nothing

    lax.fori_loop(0, (high - low) // together, several, 0)


def attend(query_vectors, own_pair, buffers, bias, carry, last, low, high, name):
    row_count = query_vectors.shape[0]
    own = own_pair is not None
    first = carry is None
    operands = [query_vectors] + (list(own_pair) if own else list(buffers) + [bias])
    operands += [] if first else list(carry)
    count = row_count if own else bias.shape[0]
    width = (high - low) * HEAD_DIM
    if last:
        shapes = [jax.ShapeDtypeStruct((row_count, width), BF16)]
    else:
        shapes = [
            jax.ShapeDtypeStruct((high - low, 8, row_count), F32),
            jax.ShapeDtypeStruct((high - low, HEAD_DIM, row_count), F32),
        ]
    held = pl.BlockSpec(memory_space=pltpu.VMEM)
    scale = {"own": 0, "early": 1, "first": 1}.get(name, 1)
    return pl.pallas_call(
        lambda *refs: attend_kernel(
            *refs, buffers=len(buffers), own=own, first=first, last=last, low=low, high=high
        ),
        in_specs=[held] * len(operands),
        out_specs=[held] * len(shapes),
        out_shape=shapes,
        name=name,
        compiler_params=pltpu.CompilerParams(vmem_limit_bytes=16 << 20),
        cost_estimate=pl.CostEstimate(
            flops=scale * 4 * row_count * count * width,
            bytes_accessed=scale * 8 * row_count * width,
            transcendentals=scale * row_count * count * (high - low),
        ),
    )(*operands)


def per_device(query_vectors, key_vectors, value_vectors, band_table, out_weight):
    row_count, width = query_vectors.shape
    block_count = lax.axis_size("tm")
    group_count = lax.axis_size("head")
    my_block = lax.axis_index("tm")
    my_group = lax.axis_index("head")
    table_row = lax.dynamic_index_in_dim(band_table, my_block, 0, keepdims=False)

    def move(array, block_to, group_to=lambda h: h):
        route = []
        for t in range(block_count):
            for h in range(group_count):
                to = block_to(t)
                if to is not None and 0 <= to < block_count:
                    route.append((t * group_count + h, to * group_count + group_to(h)))
        return lax.ppermute(array, AXES, route)

    def bias_of(pieces):
        blocks = jnp.stack([jnp.asarray(block, jnp.int32) for block, _, _ in pieces])
        number = np.concatenate([np.full(n, i) for i, (_, _, n) in enumerate(pieces)])
        rank = np.concatenate([np.arange(a, a + n) for _, a, n in pieces]).astype(np.int32)
        member = jnp.asarray(number[None, :] == np.arange(len(pieces))[:, None])
        here = jnp.arange(block_count, dtype=jnp.int32)[None, :] == blocks[:, None]
        band = jnp.sum(jnp.where(here, table_row[None, :], 0), axis=1)
        kept = jnp.where(jnp.any(here, axis=1), jnp.right_shift(jnp.int32(row_count), band), 0)
        limit = jnp.sum(jnp.where(member, kept[:, None], 0), axis=0)
        bias = jnp.where(jnp.asarray(rank) < limit, 0.0, MASKED).astype(F32)
        return jnp.broadcast_to(bias[:, None], (rank.size, HEAD_DIM))

    def within(block):
        return (block >= 0) & (block < block_count)

    head_count = width // HEAD_DIM
    core = lambda h: h ^ 1
    same = lambda t: t
    mine = my_group % 2
    level = my_group // 2
    out_width = out_weight.shape[1] // group_count
    away, home = (2 * (1 - level) + mine, 2 * level + mine)
    moved = move(out_weight, same, core)
    near = row_count // 2
    own_pair = (key_vectors, value_vectors)

    def further(buffers, pieces, carry, name):
        return attend(
            query_vectors, None, buffers, bias_of(pieces), carry, False, 0, head_count, name
        )

    def blocks_of(*sources):
        return [
            lax.dynamic_slice_in_dim(source, number * out_width, out_width, 1)
            for source in sources
            for number in (away, home)
        ]

    if block_count == 8:
        a, ab = (row_count // 8, row_count // 4)
        side = jnp.where(my_block % 2 == 0, 1, -1)
        far_of = lambda t: t - 2 if t % 2 == 0 else t + 2
        near_of = lambda t: t + 2 if t % 2 == 0 else t - 2
        twin_if = lambda source: lambda t: t ^ 1 if 0 <= source(t) < block_count else None
        ends = (0, 1, block_count - 2, block_count - 1)
        partner, two, opposite = (my_block ^ 1, my_block ^ 4, my_block ^ 6)
        far_block, near_block = (my_block - 2 * side, my_block + 2 * side)
        adjacent, far_cross = (my_block - side, my_block + 3 * side)
        at_end = (my_block < 2) | (my_block >= block_count - 2)
        three = jnp.where(at_end, opposite, -1)

        sent, sent_ab, sent_ba, sent_a = pack(
            key_vectors, value_vectors, [(0, near), (0, ab), (0, ab), (0, a)]
        )
        x_rows = move(sent, lambda t: t ^ 1)
        z_far = move(sent_ab, near_of)
        z_near = move(sent_ba, far_of)
        z_two = move(sent_a, lambda t: t ^ 4)
        carry = attend(query_vectors, own_pair, [], None, None, False, 0, head_count, "own")
        state, out_weight = lax.optimization_barrier((carry[0], out_weight))
        weights = blocks_of(out_weight)
        z_far, z_near, state, weights = lax.optimization_barrier((z_far, z_near, state, weights))
        carry = further(
            [z_far, z_near],
            [(far_block, 0, ab), (near_block, 0, ab)],
            (state, carry[1]),
            "early",
        )
        x_rows, z_near, z_two, state, weights, moved = lax.optimization_barrier(
            (x_rows, z_near, z_two, carry[0], weights, moved)
        )
        near_b = move(x_rows[:, a:ab], near_of)
        near_c = move(x_rows[:, ab:], near_of)
        cross_far = move(z_far, twin_if(far_of))
        cross_two = move(jnp.concatenate([z_near[:, :a], z_two], axis=1), lambda t: t ^ 1)
        z_three = move(z_two, lambda t: {4: 6, 5: 7, 2: 0, 3: 1}.get(t))
        carry = further(
            [x_rows, z_two],
            [(partner, 0, near), (two, 0, a)],
            (state, carry[1]),
            "first",
        )
        near_b, z_three, state, moved = lax.optimization_barrier(
            (near_b, z_three, carry[0], moved)
        )
        weights = weights + blocks_of(moved)
        chain_b = move(near_b, near_of)
        cross_three = move(z_three, lambda t: t ^ 1 if t in ends else None)
        cross_two, state, weights = lax.optimization_barrier((cross_two, state, weights))
        carry = further(
            [near_b, z_three, cross_far, cross_two],
            [
                (adjacent, a, ab - a),
                (three, 0, a),
                (far_cross, 0, ab),
                (adjacent, 0, a),
                (two ^ 1, 0, a),
            ],
            (state, carry[1]),
            "middle",
        )
        buffers = [near_c, cross_three, chain_b]
        pieces = [
            (adjacent, ab, near - ab),
            (jnp.where(at_end, opposite ^ 1, -1), 0, a),
            (my_block - 3 * side, a, ab - a),
        ]
    else:
        (packed,) = pack(key_vectors, value_vectors, [(0, near)])
        received, pieces = ([], [])
        for distance in range(1, block_count):
            rows = row_count >> distance.bit_length()
            for sign in (1, -1):
                received.append(move(packed[:, :rows], lambda t: t + sign * distance))
                pieces.append((my_block - sign * distance, 0, rows))
        carry = attend(query_vectors, own_pair, [], None, None, False, 0, head_count, "own")
        carry = further([jnp.concatenate(received[:2], axis=1)], pieces[:2], carry, "first")
        buffers, pieces = ([jnp.concatenate(received[2:], axis=1)], pieces[2:])
        weights = lax.optimization_barrier(blocks_of(out_weight, moved))

    bias = bias_of(pieces)
    cut = 2 * (head_count // 4)
    parts = []
    for low, high in ((0, cut), (cut, head_count)):
        (part,) = attend(
            query_vectors, None, buffers, bias, carry, True, low, high, f"last{low}"
        )
        parts.append((part, move(part, same, core), low * HEAD_DIM, high * HEAD_DIM))

    def project(index, first, last):
        total = 0.0
        for part, other, low, high in parts:
            total = total + jnp.dot(
                part, weights[index][low:high, first:last], preferred_element_type=F32
            )
            total = total + jnp.dot(
                other, weights[index + 2][low:high, first:last], preferred_element_type=F32
            )
        return total

    half = out_width // 2
    sent = []
    for first in (0, half):
        sent.append(project(0, first, first + half).astype(BF16))
        _, held = lax.optimization_barrier((sent[-1], [part[:2] for part in parts]))
        parts = [kept + part[2:] for kept, part in zip(held, parts)]
    arrived = [move(block, same, lambda h: h ^ 2) for block in sent]
    kept, arrived[0] = lax.optimization_barrier((project(1, 0, out_width), arrived[0]))
    return (kept + jnp.concatenate(arrived, axis=1).astype(F32)).astype(BF16)


def solution(mesh):
    in_specs = (P("tm", "head"), P("tm", "head"), P("tm", "head"), P(), P("head", None))
    out_specs = P("tm", "head")
    return jax.shard_map(
        per_device, mesh=mesh, in_specs=in_specs, out_specs=out_specs, check_vma=False
    )
```

```python
import math

import jax
import jax.numpy as jnp
import numpy as np
from jax import lax
from jax.experimental import pallas as pl
from jax.experimental.pallas import tpu as pltpu
from jax.sharding import PartitionSpec as P

HEAD_DIM = 128
MASKED = -1e30
AXES = ("tm", "head")
F32 = jnp.float32
BF16 = jnp.bfloat16


def pack_kernel(key_ref, value_ref, *out_refs, cuts):
    row_count = key_ref.shape[0]
    picks = row_count // 2
    rank = lax.broadcasted_iota(jnp.int32, (picks, 1), 0)
    place = jnp.zeros_like(rank)
    step = 1
    while step < picks:
        stride = row_count // (2 * step)
        place = jnp.where(rank >= step, (2 * (rank - step) + 1) * stride, place)
        step *= 2
    column = lax.broadcasted_iota(jnp.int32, (picks, row_count), 1)
    choose = jnp.where(place == column, 1.0, 0.0).astype(BF16)
    for plane, source in enumerate((key_ref, value_ref)):
        picked = jnp.dot(choose, source[...], preferred_element_type=F32).astype(BF16)
        for out_ref, (low, high) in zip(out_refs, cuts):
            out_ref[plane] = picked[low:high]


def pack(key_vectors, value_vectors, cuts):
    row_count, width = key_vectors.shape
    tile = width // 2
    return pl.pallas_call(
        lambda *refs: pack_kernel(*refs, cuts=cuts),
        grid=(width // tile,),
        in_specs=[pl.BlockSpec((row_count, tile), lambda j: (0, j))] * 2,
        out_specs=[
            pl.BlockSpec((2, high - low, tile), lambda j: (0, 0, j)) for low, high in cuts
        ],
        out_shape=[jax.ShapeDtypeStruct((2, high - low, width), BF16) for low, high in cuts],
        name="pack",
        compiler_params=pltpu.CompilerParams(vmem_limit_bytes=48 << 20),
        cost_estimate=pl.CostEstimate(
            flops=2 * row_count * row_count * width,
            bytes_accessed=8 * row_count * width,
            transcendentals=0,
        ),
    )(key_vectors, value_vectors)


def attend_kernel(*refs, buffers, own, first, last, low, high):
    refs = list(refs)
    query_ref = refs.pop(0)
    own_refs = [refs.pop(0), refs.pop(0)] if own else None
    packed_refs = [refs.pop(0) for _ in range(buffers)]
    bias_ref = refs.pop(0) if buffers else None
    state_in, accum_in = (None, None) if first else (refs.pop(0), refs.pop(0))
    query_count = query_ref.shape[0]
    factor = math.log2(math.e) / math.sqrt(HEAD_DIM)
    together = 2

    def one(head):
        span = pl.ds(pl.multiple_of((head + low) * HEAD_DIM, HEAD_DIM), HEAD_DIM)
        if own:
            key, value = (own_refs[0][:, span], own_refs[1][:, span])
        else:
            key = jnp.concatenate([ref[0, :, span] for ref in packed_refs], axis=0)
            value = jnp.concatenate([ref[1, :, span] for ref in packed_refs], axis=0)
        scores = lax.dot_general(
            key, query_ref[:, span], (((1,), (1,)), ((), ())), preferred_element_type=F32
        )
        if buffers:
            scores = scores + jnp.concatenate([bias_ref[...]] * (query_count // HEAD_DIM), axis=1)
        top = jnp.max(scores, axis=0, keepdims=True)
        if not first:
            state = state_in[head + low]
            top = jnp.maximum(top, state[0:1])
            shrink = jnp.exp2((state[0:1] - top) * factor)
        weights = jnp.exp2(scores * factor - top * factor)
        total = jnp.sum(weights, axis=0, keepdims=True)
        accum = jnp.dot(value.T, weights.astype(BF16), preferred_element_type=F32)
        if not first:
            total = total + shrink * state[1:2]
            accum = accum + shrink * accum_in[head + low]
        if last:
            out = pl.ds(pl.multiple_of(head * HEAD_DIM, HEAD_DIM), HEAD_DIM)
            refs[0][:, out] = (accum / total).T.astype(BF16)
        else:
            refs[0][head, 0:1, :] = top
            refs[0][head, 1:2, :] = total
            refs[1][head] = accum

    def several(step, nothing):
        for member in range(together):
            one(step * together + member)
        return nothing

    lax.fori_loop(0, (high - low) // together, several, 0)


def attend(query_vectors, own_pair, buffers, bias, carry, last, low, high, name):
    row_count = query_vectors.shape[0]
    own = own_pair is not None
    first = carry is None
    operands = [query_vectors] + (list(own_pair) if own else list(buffers) + [bias])
    operands += [] if first else list(carry)
    count = row_count if own else bias.shape[0]
    width = (high - low) * HEAD_DIM
    if last:
        shapes = [jax.ShapeDtypeStruct((row_count, width), BF16)]
    else:
        shapes = [
            jax.ShapeDtypeStruct((high - low, 8, row_count), F32),
            jax.ShapeDtypeStruct((high - low, HEAD_DIM, row_count), F32),
        ]
    held = pl.BlockSpec(memory_space=pltpu.VMEM)
    scale = {"own": 0, "early": 1, "first": 1}.get(name, 1)
    return pl.pallas_call(
        lambda *refs: attend_kernel(
            *refs, buffers=len(buffers), own=own, first=first, last=last, low=low, high=high
        ),
        in_specs=[held] * len(operands),
        out_specs=[held] * len(shapes),
        out_shape=shapes,
        name=name,
        compiler_params=pltpu.CompilerParams(vmem_limit_bytes=16 << 20),
        cost_estimate=pl.CostEstimate(
            flops=scale * 4 * row_count * count * width,
            bytes_accessed=scale * 8 * row_count * width,
            transcendentals=scale * row_count * count * (high - low),
        ),
    )(*operands)


def per_device(query_vectors, key_vectors, value_vectors, band_table, out_weight):
    row_count, width = query_vectors.shape
    block_count = lax.axis_size("tm")
    group_count = lax.axis_size("head")
    my_block = lax.axis_index("tm")
    my_group = lax.axis_index("head")
    table_row = lax.dynamic_index_in_dim(band_table, my_block, 0, keepdims=False)

    def move(array, block_to, group_to=lambda h: h):
        route = []
        for t in range(block_count):
            for h in range(group_count):
                to = block_to(t)
                if to is not None and 0 <= to < block_count:
                    route.append((t * group_count + h, to * group_count + group_to(h)))
        return lax.ppermute(array, AXES, route)

    def bias_of(pieces):
        blocks = jnp.stack([jnp.asarray(block, jnp.int32) for block, _, _ in pieces])
        number = np.concatenate([np.full(n, i) for i, (_, _, n) in enumerate(pieces)])
        rank = np.concatenate([np.arange(a, a + n) for _, a, n in pieces]).astype(np.int32)
        member = jnp.asarray(number[None, :] == np.arange(len(pieces))[:, None])
        here = jnp.arange(block_count, dtype=jnp.int32)[None, :] == blocks[:, None]
        band = jnp.sum(jnp.where(here, table_row[None, :], 0), axis=1)
        kept = jnp.where(jnp.any(here, axis=1), jnp.right_shift(jnp.int32(row_count), band), 0)
        limit = jnp.sum(jnp.where(member, kept[:, None], 0), axis=0)
        bias = jnp.where(jnp.asarray(rank) < limit, 0.0, MASKED).astype(F32)
        return jnp.broadcast_to(bias[:, None], (rank.size, HEAD_DIM))

    def within(block):
        return (block >= 0) & (block < block_count)

    head_count = width // HEAD_DIM
    core = lambda h: h ^ 1
    same = lambda t: t
    mine = my_group % 2
    level = my_group // 2
    out_width = out_weight.shape[1] // group_count
    away, home = (2 * (1 - level) + mine, 2 * level + mine)
    moved = move(out_weight, same, core)
    near = row_count // 2
    own_pair = (key_vectors, value_vectors)

    def further(buffers, pieces, carry, name):
        return attend(
            query_vectors, None, buffers, bias_of(pieces), carry, False, 0, head_count, name
        )

    def block_of(source, number):
        return lax.dynamic_slice_in_dim(source, number * out_width, out_width, 1)

    if block_count == 8:
        a, ab = (row_count // 8, row_count // 4)
        side = jnp.where(my_block % 2 == 0, 1, -1)
        far_of = lambda t: t - 2 if t % 2 == 0 else t + 2
        near_of = lambda t: t + 2 if t % 2 == 0 else t - 2
        twin_if = lambda source: lambda t: t ^ 1 if 0 <= source(t) < block_count else None
        ends = (0, 1, block_count - 2, block_count - 1)
        partner, two, opposite = (my_block ^ 1, my_block ^ 4, my_block ^ 6)
        far_block, near_block = (my_block - 2 * side, my_block + 2 * side)
        adjacent, far_cross = (my_block - side, my_block + 3 * side)
        at_end = (my_block < 2) | (my_block >= block_count - 2)
        three = jnp.where(at_end, opposite, -1)

        sent, sent_ab, sent_ba, sent_a = pack(
            key_vectors, value_vectors, [(0, near), (0, ab), (0, ab), (0, a)]
        )
        x_rows = move(sent, lambda t: t ^ 1)
        z_far = move(sent_ab, near_of)
        z_near = move(sent_ba, far_of)
        z_two = move(sent_a, lambda t: t ^ 4)
        carry = attend(query_vectors, own_pair, [], None, None, False, 0, head_count, "own")
        state, out_weight = lax.optimization_barrier((carry[0], out_weight))
        weights = [block_of(out_weight, away), block_of(out_weight, home)]
        z_far, z_near, state, weights = lax.optimization_barrier((z_far, z_near, state, weights))
        carry = further(
            [z_far, z_near],
            [(far_block, 0, ab), (near_block, 0, ab)],
            (state, carry[1]),
            "early",
        )
        x_rows, z_near, z_two, state, moved = lax.optimization_barrier(
            (x_rows, z_near, z_two, carry[0], moved)
        )
        near_b = move(x_rows[:, a:ab], near_of)
        near_c = move(x_rows[:, ab:], near_of)
        cross_far = move(z_far, twin_if(far_of))
        cross_two = move(jnp.concatenate([z_near[:, :a], z_two], axis=1), lambda t: t ^ 1)
        z_three = move(z_two, lambda t: {4: 6, 5: 7, 2: 0, 3: 1}.get(t))
        carry = further(
            [x_rows, z_two],
            [(partner, 0, near), (two, 0, a)],
            (state, carry[1]),
            "first",
        )
        near_b, z_three, state, moved = lax.optimization_barrier(
            (near_b, z_three, carry[0], moved)
        )
        weights = [weights[0], block_of(moved, away), weights[1]]
        chain_b = move(near_b, near_of)
        cross_three = move(z_three, lambda t: t ^ 1 if t in ends else None)
        near_c, state, weights = lax.optimization_barrier((near_c, state, weights))
        carry = further(
            [near_b, near_c, z_three, cross_far],
            [
                (adjacent, a, ab - a),
                (adjacent, ab, near - ab),
                (three, 0, a),
                (far_cross, 0, ab),
            ],
            (state, carry[1]),
            "middle",
        )
        buffers = [cross_two, cross_three, chain_b]
        pieces = [
            (adjacent, 0, a),
            (two ^ 1, 0, a),
            (jnp.where(at_end, opposite ^ 1, -1), 0, a),
            (my_block - 3 * side, a, ab - a),
        ]
    else:
        (packed,) = pack(key_vectors, value_vectors, [(0, near)])
        received, pieces = ([], [])
        for distance in range(1, block_count):
            rows = row_count >> distance.bit_length()
            for sign in (1, -1):
                received.append(move(packed[:, :rows], lambda t: t + sign * distance))
                pieces.append((my_block - sign * distance, 0, rows))
        carry = attend(query_vectors, own_pair, [], None, None, False, 0, head_count, "own")
        carry = further([jnp.concatenate(received[:2], axis=1)], pieces[:2], carry, "first")
        buffers, pieces = ([jnp.concatenate(received[2:], axis=1)], pieces[2:])
        weights = lax.optimization_barrier(
            [block_of(out_weight, away), block_of(moved, away), block_of(out_weight, home)]
        )

    bias = bias_of(pieces)
    cut = 2 * (head_count // 4)
    parts = []
    for low, high in ((0, cut), (cut, head_count)):
        (part,) = attend(
            query_vectors, None, buffers, bias, carry, True, low, high, f"last{low}"
        )
        parts.append((part, move(part, same, core), low * HEAD_DIM, high * HEAD_DIM))

    def project(first, last):
        total = 0.0
        for part, other, low, high in parts:
            total = total + jnp.dot(
                part, weights[0][low:high, first:last], preferred_element_type=F32
            )
            total = total + jnp.dot(
                other, weights[1][low:high, first:last], preferred_element_type=F32
            )
        return total

    half = out_width // 2
    sent = []
    for first in (0, half):
        sent.append(project(first, first + half).astype(BF16))
        _, held, moved = lax.optimization_barrier(
            (sent[-1], [part[:2] for part in parts], moved)
        )
        parts = [kept + part[2:] for kept, part in zip(held, parts)]
    arrived = [move(block, same, lambda h: h ^ 2) for block in sent]
    weights = [weights[2], block_of(moved, home)]
    kept, arrived[0] = lax.optimization_barrier((project(0, out_width), arrived[0]))
    return (kept + jnp.concatenate(arrived, axis=1).astype(F32)).astype(BF16)


def solution(mesh):
    in_specs = (P("tm", "head"), P("tm", "head"), P("tm", "head"), P(), P("head", None))
    out_specs = P("tm", "head")
    return jax.shard_map(
        per_device, mesh=mesh, in_specs=in_specs, out_specs=out_specs, check_vma=False
    )
```
